512 devices in a mesh: bead: 64 (over z, y), slab: 8 (over x, core).
Axes of the slice: x: 4, y: 4, z: 16, core: 2. Of those that a mesh axis runs over, the one named last changes fastest.
Arguments:
- positions: float32 [3, 64, 1024], P(None, 'bead', 'slab'), may hold values from -5 to 5
- velocities: float32 [3, 64, 1024], P(None, 'bead', 'slab'), may hold values from -5 to 5
- atom_types: int32 [1024], P('slab'), may hold values from 0 to 1
- live_atoms: int32 [8], P('slab'), may hold values from 16 to 128, as said below
- halo_rows: int32 [8, 128], P('slab'), may hold values from 0 to 127, as said below
- neighbours: int32 [1024, 128], P('slab'), may hold values from -1 to 255, as said below
- type_scale: float32 [2, 25], replicated, may hold values from -4 to 4
- type_shift: float32 [2, 25], replicated, may hold values from -4 to 4
- embed_two: bfloat16 [25, 50], replicated, may hold values from -1.25 to 1.25
- embed_bias_two: float32 [50], replicated, may hold values from -3 to 3
- embed_three: bfloat16 [50, 100], replicated, may hold values from -0.875 to 0.875
- embed_bias_three: float32 [100], replicated, may hold values from -3 to 3
- fit_first: bfloat16 [1600, 240], replicated, may hold values from -0.625 to 0.625
- fit_bias_first: float32 [240], replicated, may hold values from -3 to 3
- fit_second: bfloat16 [240, 240], replicated, may hold values from -0.375 to 0.375
- fit_bias_second: float32 [240], replicated, may hold values from -3 to 3
- fit_third: bfloat16 [240, 240], replicated, may hold values from -0.375 to 0.375
- fit_bias_third: float32 [240], replicated, may hold values from -3 to 3
- fit_readout: float32 [2, 240], replicated, may hold values from -0.375 to 0.375
Outputs:
- positions_new: float32 [3, 64, 1024], P(None, 'bead', 'slab')
- velocities_new: float32 [3, 64, 1024], P(None, 'bead', 'slab')
- forces: float32 [3, 64, 1024], P(None, 'bead', 'slab')
The draws below stay inside these ranges and needn't reach their ends.
Inputs may be any that keep to these rules, and one draw needn't show every extreme that they name: Slab s holds atoms in its first live_atoms[s] rows; one slab is full. The system is a water film with vacuum on both sides, so slabs crossing the vacuum hold few atoms. `halo_rows`: each entry is an occupied row of its slab; the first 64 of a slab go to the slab one lower (cyclic), the other 64 to the slab one higher. `neighbours`: -1 marks an empty slot; entries below 128 are occupied own rows of the slab, never the atom itself; entries from 128 on index the extended list's halo part. Rows at or past a slab's live count are all empty; an occupied row has between 64 and 128 filled slots, first, and some row of each slab has 128.
All inputs are finite; a program needn't handle non-finite values.
Results may differ from the reference program's by a relative error of at most 0.014.
Values sent between devices are 32-bit elements; how exact they have to be, the bound alone decides.
A program may use at most 64 MiB of HBM per device.

```python
import jax
import jax.numpy as jnp
from jax import lax

E1 = 25
E2 = 50
E3 = 100
M2 = 16
FIT = 240
NEIGH = 128
BLOCK = 32
ATOMS_DEV = 128
HALO = 64
ATOMS = 1024
BEADS = 64
N_SLAB = 8


def slab_live(key):
    slab_total = ATOMS // ATOMS_DEV
    spread = jax.random.randint(jax.random.fold_in(key, 101), (slab_total,), ATOMS_DEV // 8, ATOMS_DEV // 2 + 1)
    fullest = jax.random.randint(jax.random.fold_in(key, 102), (), 0, slab_total)
    return jnp.where(jnp.arange(slab_total) == fullest, ATOMS_DEV, spread).astype(jnp.int32)


def draw_live_atoms(key, part):
    return slab_live(key)


def draw_halo_rows(key, part):
    living = slab_live(key)
    slab_total = living.shape[0]
    return jax.random.randint(jax.random.fold_in(key, 103), (slab_total, 2 * HALO), 0, living[:, None]).astype(jnp.int32)


def draw_neighbours(key, part):
    living = slab_live(key)
    slab_total = living.shape[0]
    atom_rows = jnp.arange(ATOMS_DEV)[None, :]
    listed = jax.random.randint(jax.random.fold_in(key, 104), (slab_total, ATOMS_DEV), NEIGH // 2, NEIGH + 1)
    listed = jnp.where(atom_rows == 0, NEIGH, listed)
    listed = jnp.where(atom_rows < living[:, None], listed, 0)
    live_wide = living[:, None, None]
    chosen = jax.random.randint(jax.random.fold_in(key, 105), (slab_total, ATOMS_DEV, NEIGH), 0, live_wide + 2 * HALO)
    own_row = atom_rows[:, :, None]
    chosen = jnp.where(chosen == own_row, (own_row + 1) % live_wide, chosen)
    entries = jnp.where(chosen < live_wide, chosen, ATOMS_DEV + chosen - live_wide)
    slot_index = jnp.arange(NEIGH)[None, None, :]
    entries = jnp.where(slot_index < listed[:, :, None], entries, -1)
    return entries.reshape(slab_total * ATOMS_DEV, NEIGH).astype(jnp.int32)


def touch_ends(result, own_key, low, top_value):
    index_at = [jax.random.randint(jax.random.fold_in(own_key, axis), (), 0, length) for axis, length in enumerate(result.shape)]
    main_axis = result.shape.index(max(result.shape))
    neighbour = index_at[:main_axis] + [(index_at[main_axis] + 1) % result.shape[main_axis]] + index_at[main_axis + 1:]
    return result.at[tuple(index_at)].set(low).at[tuple(neighbour)].set(top_value)


def level_of(rng, extent, pieces, least, top_value):
    level = 1.0
    for dim, shards_of in pieces:
        draws = jax.random.uniform(jax.random.fold_in(jax.random.fold_in(rng, 6), dim), (shards_of,), jnp.float32, least / len(pieces), top_value / len(pieces))
        level = level * jnp.repeat(jnp.exp(draws), extent[dim] // shards_of).reshape((-1,) + (1,) * (len(extent) - 1 - dim))
    return level


def normal_values(key, shape, scale, limit, cuts=(), held_as=jnp.bfloat16):
    array = jax.random.normal(key, shape, jnp.float32) * scale
    if len(cuts) > 0:
        array = level_of(key, shape, cuts, -0.22, 0.18) * array
    return jnp.clip(array, min=-limit, max=limit).astype(held_as)


def setup_inputs(seed: int = 0) -> dict:
    arg_keys = jax.random.split(jax.random.key(seed), 20)
    return {
        "positions": normal_values(arg_keys[0], (3, BEADS, ATOMS), 1.0, 5.0, ((1, 64), (2, 8)), jnp.float32),
        "velocities": normal_values(arg_keys[1], (3, BEADS, ATOMS), 1.0, 5.0, ((1, 64), (2, 8)), jnp.float32),
        "atom_types": touch_ends(jax.random.randint(arg_keys[2], (ATOMS,), 0, 2), jax.random.fold_in(arg_keys[2], 1), 0, 1).astype(jnp.int32),
        "live_atoms": draw_live_atoms(jax.random.fold_in(arg_keys[19], 71), 0),
        "halo_rows": draw_halo_rows(jax.random.fold_in(arg_keys[19], 71), 0),
        "neighbours": draw_neighbours(jax.random.fold_in(arg_keys[19], 71), 0),
        "type_scale": normal_values(arg_keys[6], (2, E1), 1.0, 4.0, (), jnp.float32),
        "type_shift": normal_values(arg_keys[7], (2, E1), 1.0, 4.0, (), jnp.float32),
        "embed_two": normal_values(arg_keys[8], (E1, E2), E1 ** -0.5, 1.25),
        "embed_bias_two": normal_values(arg_keys[9], (E2,), 0.5, 3.0, (), jnp.float32),
        "embed_three": normal_values(arg_keys[10], (E2, E3), E2 ** -0.5, 0.875),
        "embed_bias_three": normal_values(arg_keys[11], (E3,), 0.5, 3.0, (), jnp.float32),
        "fit_first": normal_values(arg_keys[12], (E3 * M2, FIT), (E3 * M2 // 16) ** -0.5, 0.625),
        "fit_bias_first": normal_values(arg_keys[13], (FIT,), 0.5, 3.0, (), jnp.float32),
        "fit_second": normal_values(arg_keys[14], (FIT, FIT), FIT ** -0.5, 0.375),
        "fit_bias_second": normal_values(arg_keys[15], (FIT,), 0.5, 3.0, (), jnp.float32),
        "fit_third": normal_values(arg_keys[16], (FIT, FIT), FIT ** -0.5, 0.375),
        "fit_bias_third": normal_values(arg_keys[17], (FIT,), 0.5, 3.0, (), jnp.float32),
        "fit_readout": normal_values(arg_keys[18], (2, FIT), FIT ** -0.5, 0.375, (), jnp.float32),
    }


step_size = 0.25
phase_rate = 1.2
cutoff_sq = 16.0
softening = 0.25
heavy_mass = 16.0
highest = lax.Precision.HIGHEST

def mode_tables(bead_count):
    indices = jnp.arange(bead_count)
    bead_rows = indices[:, None].astype(jnp.float32)
    mode_cols = indices[None, :]
    mode_float = mode_cols.astype(jnp.float32)
    angles = 2.0 * jnp.pi * bead_rows * mode_float / bead_count
    norm_scale = jnp.sqrt(2.0 / bead_count)
    middle = bead_count // 2
    edge_value = 1.0 / jnp.sqrt(1.0 * bead_count)
    mode_basis = jnp.where(mode_cols == 0, edge_value, jnp.where(mode_cols < middle, norm_scale * jnp.cos(angles), jnp.where(mode_cols == middle, jnp.cos(jnp.pi * bead_rows) * edge_value, norm_scale * jnp.sin(angles))))
    sine_part = jnp.sin(jnp.pi * indices.astype(jnp.float32) / bead_count)
    ratio = 2.0 * sine_part
    phases = phase_rate * bead_count * sine_part
    guarded = jnp.where(indices == 0, 1.0, ratio)
    cosine = jnp.cos(phases)
    travel = jnp.where(indices == 0, 1.0, jnp.sin(phases) / guarded)
    spring = ratio * jnp.sin(phases)
    return (mode_basis, cosine, travel, spring)

def bead_matrices(bead_count):
    mode_basis, cosine, travel, spring = mode_tables(bead_count)

    def assemble(diagonal):
        return jnp.dot(mode_basis * diagonal[None, :], mode_basis.T, preferred_element_type=jnp.float32, precision=highest)
    return (assemble(cosine), assemble(travel), assemble(spring))

def block_energy(centre, beside_all, around_hydrogen, filled, centre_hydrogen, living, weights):
    type_scale, type_shift, embed_two, embed_bias_two, embed_three, embed_bias_three, fit_first, fit_bias_first, fit_second, fit_bias_second, fit_third, fit_bias_third, fit_readout = weights
    offsets = beside_all - centre[:, :, None]
    dist_sq = lax.optimization_barrier(jnp.sum(offsets * offsets, axis=0))
    softened = jnp.sqrt(dist_sq + softening)
    switch = jnp.maximum(1.0 - dist_sq / cutoff_sq, 0.0)
    strength = filled * switch * switch / softened
    environ = jnp.concatenate([strength[None], strength[None] * offsets / softened[None]], axis=0)
    block_rows, slot_count = strength.shape
    input_scale = type_scale[0] + around_hydrogen[..., None] * (type_scale[1] - type_scale[0])
    input_shift = type_shift[0] + around_hydrogen[..., None] * (type_shift[1] - type_shift[0])
    layer_one = jnp.tanh(strength[..., None] * input_scale + input_shift).reshape(block_rows * slot_count, -1)
    layer_two = jnp.tanh(jnp.dot(layer_one.astype(jnp.bfloat16), embed_two, preferred_element_type=jnp.float32) + embed_bias_two)
    layer_two = layer_two + jnp.concatenate([layer_one, layer_one], axis=1)
    layer_three = jnp.tanh(jnp.dot(layer_two.astype(jnp.bfloat16), embed_three, preferred_element_type=jnp.float32) + embed_bias_three)
    layer_three = layer_three + jnp.concatenate([layer_two, layer_two], axis=1)
    layer_three = layer_three.reshape(block_rows, slot_count, -1)
    features = jnp.einsum('bke,cbk->bec', layer_three, environ, precision=highest) / slot_count
    descriptor = jnp.einsum('bec,bfc->bef', features, features[:, :M2], precision=highest).reshape(block_rows, -1)
    fit_one = jnp.tanh(jnp.dot(descriptor.astype(jnp.bfloat16), fit_first, preferred_element_type=jnp.float32) + fit_bias_first)
    fit_two = jnp.tanh(jnp.dot(fit_one.astype(jnp.bfloat16), fit_second, preferred_element_type=jnp.float32) + fit_bias_second) + fit_one
    fit_three = jnp.tanh(jnp.dot(fit_two.astype(jnp.bfloat16), fit_third, preferred_element_type=jnp.float32) + fit_bias_third) + fit_two
    readout = fit_readout[0] + centre_hydrogen[:, None] * (fit_readout[1] - fit_readout[0])
    return jnp.sum(living * lax.optimization_barrier(jnp.sum(fit_three * readout, axis=1)))

def slab_gradient(extended, wide_hydrogen, slab_lists, live_count, block_count, weights):

    def add_block(block_index, gradient):
        first_row = block_index * BLOCK
        centre = lax.dynamic_slice_in_dim(extended, first_row, BLOCK, 1)
        listed = lax.dynamic_slice_in_dim(slab_lists, first_row, BLOCK, 0)
        filled = (listed >= 0).astype(jnp.float32)
        flat_rows = jnp.where(listed >= 0, listed, 0).reshape(-1).astype(jnp.int32)
        beside_all = extended[:, flat_rows].reshape(3, BLOCK, -1)
        around_hydrogen = wide_hydrogen[flat_rows].reshape(BLOCK, -1)
        centre_hydrogen = lax.dynamic_slice_in_dim(wide_hydrogen, first_row, BLOCK, 0)
        row_numbers = first_row + jnp.arange(BLOCK).astype(jnp.int32)
        living = (row_numbers < live_count).astype(jnp.float32)

        def energy_of(centre_in, around_in):
            return block_energy(centre_in, around_in, around_hydrogen, filled, centre_hydrogen, living, weights)
        energy, backward = jax.vjp(energy_of, centre, beside_all)
        grad_centre, grad_around = backward(jnp.ones_like(energy))
        gradient = gradient.at[:, flat_rows].add(grad_around.reshape(3, -1))
        current = lax.dynamic_slice_in_dim(gradient, first_row, BLOCK, 1)
        return lax.dynamic_update_slice_in_dim(gradient, current + grad_centre, first_row, 1)
    zeroed = jnp.zeros(extended.shape, jnp.float32)
    return lax.fori_loop(0, block_count, add_block, zeroed)

def reference(positions, velocities, atom_types, live_atoms, halo_rows, neighbours, type_scale, type_shift, embed_two, embed_bias_two, embed_three, embed_bias_three, fit_first, fit_bias_first, fit_second, fit_bias_second, fit_third, fit_bias_third, fit_readout):
    weights = (type_scale, type_shift, embed_two, embed_bias_two, embed_three, embed_bias_three, fit_first, fit_bias_first, fit_second, fit_bias_second, fit_third, fit_bias_third, fit_readout)
    hydrogen = (atom_types == 1).astype(jnp.float32)
    gradient_total = jnp.zeros((BEADS, 3, ATOMS), jnp.float32)
    for slab_index in range(N_SLAB):
        before = (slab_index - 1) % N_SLAB
        following = (slab_index + 1) % N_SLAB
        own_rows = jnp.arange(ATOMS_DEV).astype(jnp.int32) + slab_index * ATOMS_DEV
        rows_before = halo_rows[before, HALO:].astype(jnp.int32) + before * ATOMS_DEV
        rows_after = halo_rows[following, :HALO].astype(jnp.int32) + following * ATOMS_DEV
        gathered = jnp.concatenate([own_rows, rows_before, rows_after]).astype(jnp.int32)
        wide_hydrogen = hydrogen[gathered]
        slab_lists = neighbours[slab_index * ATOMS_DEV:(slab_index + 1) * ATOMS_DEV]
        live_count = live_atoms[slab_index]
        block_count = (live_count + BLOCK - 1) // BLOCK
        bead_fields = jnp.transpose(positions[:, :, gathered], (1, 0, 2))

        def bead_force(bead_field):
            return slab_gradient(bead_field, wide_hydrogen, slab_lists, live_count, block_count, weights)
        gradients = lax.map(bead_force, bead_fields)
        gradient_total = gradient_total.at[:, :, gathered].add(gradients)
    forces = -jnp.transpose(gradient_total, (1, 0, 2))
    inverse_mass = jnp.where(atom_types == 1, 1.0, 1.0 / heavy_mass)
    kicked = velocities + step_size * inverse_mass[None, None, :] * forces
    rot_cos, rot_travel, rot_spring = bead_matrices(BEADS)
    positions_new = jnp.einsum('ij,cja->cia', rot_cos, positions, precision=highest) + jnp.einsum('ij,cja->cia', rot_travel, kicked, precision=highest)
    velocities_new = jnp.einsum('ij,cja->cia', -rot_spring, positions, precision=highest) + jnp.einsum('ij,cja->cia', rot_cos, kicked, precision=highest)
    return (positions_new, velocities_new, forces)
```

```python
import functools

import jax
import jax.numpy as jnp
import numpy as np
from jax import lax
from jax.experimental import pallas as pl
from jax.experimental.pallas import tpu as pltpu
from jax.sharding import PartitionSpec as P

BEADS = 64
N_SLAB = 8
SHARE = 16
LANES = 128
STEP = 0.25
HEAVY = 16.0
BLK = 8
CHUNK = 64
F32 = jnp.float32
BF16 = jnp.bfloat16
NT = (((1,), (1,)), ((), ()))
HIGH = lax.Precision.HIGHEST


def two_feature(row):
    if row < 24:
        return row
    if row < 48:
        return row + 1
    if row < 52:
        return (24, 49)[(row - 48) % 2]
    return -1


def three_feature(row):
    if row < 48:
        return two_feature(row)
    if row < 96:
        return 50 + two_feature(row - 48)
    if row < 100:
        return (24, 49, 74, 99)[row - 96]
    return -1


def selections():
    one_of = [k if k < 24 else 24 if k < 28 else -1 for k in range(32)]
    s1 = np.zeros((32, 25), np.float32)
    for k, f in enumerate(one_of):
        if f >= 0:
            s1[k, f] = 1
    a2 = np.zeros((56, 50), np.float32)
    for k in range(56):
        if two_feature(k) >= 0:
            a2[k, two_feature(k)] = 1
    b1 = np.zeros((25, 32), np.float32)
    for f in range(25):
        b1[f, f] = 1
    a3 = np.zeros((104, 100), np.float32)
    where = np.zeros((104,), np.int32)
    where[100:] = 127
    for k in range(104):
        if three_feature(k) >= 0:
            a3[k, three_feature(k)] = 1
            where[three_feature(k)] = k
    b2 = np.zeros((50, 56), np.float32)
    for k in range(50):
        b2[two_feature(k), k] = 1
    spread = np.full((16, LANES), 127, np.int32)
    fold = np.zeros((13 * LANES, LANES), np.float32)
    for g in range(13):
        for lane in range(LANES):
            e = 8 * g + lane // 16
            spread[g, lane] = where[e]
            if e < 100:
                fold[g * LANES + lane, where[e]] = 1
    return s1, a2, b1, a3, b2, spread, fold


def mode_matrices():
    n = BEADS
    j, k = np.arange(n)[:, None], np.arange(n)[None, :]
    angle = 2 * np.pi * ((j * k) % n) / n
    basis = np.where(
        k == 0,
        1 / np.sqrt(n),
        np.where(
            k < n // 2,
            np.sqrt(2 / n) * np.cos(angle),
            np.where(k == n // 2, np.where(j % 2 == 0, 1.0, -1.0) / np.sqrt(n), np.sqrt(2 / n) * np.sin(angle)),
        ),
    )
    sine = np.sin(np.pi * np.arange(n) / n)
    ratio = 2 * sine
    theta = 1.2 * n * sine
    travel = np.where(np.arange(n) == 0, 1.0, np.sin(theta) / np.where(np.arange(n) == 0, 1.0, ratio))
    return tuple(
        ((basis * d[None, :]) @ basis.T).astype(np.float32)
        for d in (np.cos(theta), travel, ratio * np.sin(theta))
    )


def lanes_of(table, index):
    return jnp.take_along_axis(table, index, axis=1, mode="promise_in_bounds")


def spread_rows(row, count):
    return jnp.broadcast_to(row, (count, row.shape[1]))


def own_tile(pos, types, halo):
    hydrogen = jnp.where(types == 1, 1.0, 0.0).astype(F32)
    mine = jnp.concatenate([pos, hydrogen], axis=0)
    wide = jnp.concatenate([mine, mine], axis=0)
    sent = lanes_of(wide, spread_rows(halo, 8))
    return jnp.where(lax.broadcasted_iota(jnp.int32, (8, LANES), 0) < 4, wide, sent)


def thirds(row):
    high = row.astype(BF16).astype(F32)
    rest = row - high
    mid = rest.astype(BF16).astype(F32)
    return high, mid, rest - mid


def bias_rows(bias, first, count):
    high, mid, low = thirds(bias)
    at = lax.broadcasted_iota(jnp.int32, (count, bias.shape[1]), 0)
    return jnp.where(at == first, high, jnp.where(at == first + 1, mid, jnp.where(at == first + 2, low, 0.0)))


def prepare_weights(scale, shift, w2, b2, w3, b3, s1, a2, p1, a3, p2, w2t, w3t, cols):
    dot = functools.partial(lax.dot_general, preferred_element_type=F32)
    two = dot(a2[...], w2[...], NT).astype(BF16)
    two = dot(two, p1[...], (((1,), (0,)), ((), ())))
    two = two + dot(a2[...], bias_rows(b2[...], 28, 32).astype(BF16), NT)
    w2t[...] = two.astype(BF16)
    three = dot(a3[...], w3[...], NT).astype(BF16)
    three = dot(three, p2[...], (((1,), (0,)), ((), ())))
    three = three + dot(a3[...], bias_rows(b3[...], 52, 56).astype(BF16), NT)
    w3t[...] = three.astype(BF16)
    at = lax.broadcasted_iota(jnp.int32, (32, LANES), 0)
    ones = jnp.where((at >= 28) & (at < 31), 20.0, 0.0)
    for kind in range(2):
        for n, ref in enumerate((scale, shift)):
            col = dot(s1[...], spread_rows(ref[kind : kind + 1, :], LANES), NT, precision=HIGH)
            cols[2 * n + kind] = col + ones if n else col


def force_kernel(
    tile, nb, w2t, w3t, cols, spread, fold_hbm, fit1_hbm, fit2_hbm, fit3_hbm, c1, c2, c3, readout,
    out,
    env, geo, order, count, hc, three, feats, gfeats, qs, ps, scat, fold, fit1, fit2, fit3, sems,
):
    me = lax.axis_index("slab")
    loads = [
        pltpu.make_async_copy(src, dst, sems.at[n])
        for n, (src, dst) in enumerate(
            ((fit1_hbm, fit1), (fit2_hbm, fit2), (fit3_hbm, fit3), (fold_hbm, fold))
        )
    ]
    for load in loads:
        load.start()
    dot = functools.partial(lax.dot_general, preferred_element_type=F32)
    NN = (((1,), (0,)), ((), ()))
    lane8 = lax.broadcasted_iota(jnp.int32, (8, LANES), 1)
    row8 = lax.broadcasted_iota(jnp.int32, (8, LANES), 0)

    for s in range(N_SLAB):
        count[s] = jnp.sum(jnp.where(nb[s][:, 0:1] >= 0, 1.0, 0.0)).astype(jnp.int32)
    total = jnp.int32(0)
    for s in range(N_SLAB):
        for j in range(SHARE):
            order[total + j] = s * SHARE + j
        total = total + count[s]
    for j in range(BLK):
        order[total + j] = N_SLAB * SHARE
    env[pl.ds(N_SLAB * SHARE * 8, 8), :] = jnp.zeros((8, LANES), F32)

    def own_row(s, half):
        return (row8 + half * 8) * 8 + lax.rem(me - s + N_SLAB, N_SLAB)

    def geometry(s, half):
        before = lax.rem(s + N_SLAB - 1, N_SLAB)
        after = lax.rem(s + 1, N_SLAB)
        idx = nb[s, half * 8 : half * 8 + 8, :]
        low = idx & 127
        far = idx >= 128
        own = tile[s]
        edge = pltpu.roll(jnp.where(lane8 >= 64, tile[before], tile[after]), 64, 1)
        centre_at = own_row(s, half)
        base = s * SHARE + half * 8
        got = []
        for c in range(4):
            near = lanes_of(spread_rows(own[c : c + 1], 8), low)
            there = lanes_of(spread_rows(edge[4 + c : 5 + c], 8), low)
            got.append(jnp.where(far, there, near))
        mid = [lanes_of(spread_rows(own[c : c + 1], 8), centre_at) for c in range(4)]
        off = [got[c] - mid[c] for c in range(3)]
        d2 = off[0] * off[0] + off[1] * off[1] + off[2] * off[2]
        inv = lax.rsqrt(d2 + 0.25)
        fsw = jnp.where(idx >= 0, jnp.maximum(1.0 - d2 * (1.0 / 16.0), 0.0), 0.0)
        strength = fsw * fsw * inv
        si = strength * inv
        at = pl.ds(base, 8)
        for n, value in enumerate((*off, inv, fsw)):
            geo[n, at, :] = value
        for n, value in enumerate((strength, si * off[0], si * off[1], si * off[2], got[3], mid[3])):
            env[pl.ds(base * 8 + n, 8, stride=8), :] = value

    for s in range(N_SLAB):
        geometry(s, 0)

    def second_half(fn):
        def step(s, carry):
            @pl.when(count[s] > 8)
            def _():
                fn(s, 1)
            return carry

        lax.fori_loop(0, N_SLAB, step, 0)

    second_half(geometry)

    sc0, sc1, sh0, sh1 = 0, 1, 2, 3

    def forward(block, carry):
        first = block * BLK
        e, one, done = [], [], []
        for b in range(BLK):
            row = order[first + b]
            v = env[pl.ds(pl.multiple_of(row * 8, 8), 8), :]
            e.append(v)
            hyd = v[4:5] > 0.5
            sc = jnp.where(hyd, cols[sc1], cols[sc0])
            t = jnp.tanh(v[0:1] * sc + jnp.where(hyd, cols[sh1], cols[sh0]))
            one.append((t, (1.0 - t * t) * sc))
            hc[pl.ds(first + b, 1), :] = v[5:6]
        x = jnp.concatenate([a.astype(BF16) for pair in one for a in pair], axis=1)
        z = dot(w2t[...], x, NN)
        two = []
        for b in range(BLK):
            t1, d1 = one[b]
            t = jnp.tanh(z[:, 256 * b : 256 * b + 128])
            d = (1.0 - t * t) * z[:, 256 * b + 128 : 256 * b + 256]
            two.append((
                t + jnp.concatenate([t1[:24], t1[:24], t1[24:]], axis=0),
                d + jnp.concatenate([d1[:24], d1[:24], d1[24:]], axis=0),
            ))
        x = jnp.concatenate([a.astype(BF16) for pair in two for a in pair], axis=1)
        z = dot(w3t[...], x, NN)
        for b in range(BLK):
            t2, d2 = two[b]
            t = jnp.tanh(z[:, 256 * b : 256 * b + 128])
            d = (1.0 - t * t) * z[:, 256 * b + 128 : 256 * b + 256]
            l3 = (t + jnp.concatenate([t2[:48], t2[:48], t2[48:]], axis=0)).astype(BF16)
            d3 = (d + jnp.concatenate([d2[:48], d2[:48], d2[48:]], axis=0)).astype(BF16)
            three[first + b] = jnp.concatenate([l3, d3], axis=1)
            f = dot(e[b].astype(BF16), l3, NT) * (1.0 / 128.0)
            feats[pl.ds(pl.multiple_of((first + b) * 8, 8), 8), :] = jnp.concatenate(
                [f, jnp.zeros((8, 24), F32)], axis=1
            )
        return carry

    blocks = lax.div(total + (BLK - 1), BLK)
    lax.fori_loop(0, blocks, forward, 0)

    for load in loads:
        load.wait()

    lane_m = lax.broadcasted_iota(jnp.int32, (CHUNK, LANES), 1)

    def fit(chunk, carry):
        base = chunk * (CHUNK * 8)
        fs = [feats[pl.ds(base + c, CHUNK, stride=8), :] for c in range(4)]
        tiled = [lanes_of(f, lane_m & 15) for f in fs]
        spreads = [
            [lanes_of(f, spread_rows(spread[g : g + 1, :], CHUNK)) for f in fs] for g in range(13)
        ]
        desc = [sum(spreads[g][c] * tiled[c] for c in range(4)) for g in range(13)]
        desc = jnp.concatenate(desc, axis=1).astype(BF16)[:, :1600]
        f1 = jnp.tanh(dot(desc, fit1[...], NN) + c1[...])
        t2 = jnp.tanh(dot(f1.astype(BF16), fit2[...], NN) + c2[...])
        f2 = t2 + f1
        t3 = jnp.tanh(dot(f2.astype(BF16), fit3[...], NN) + c3[...])
        h = hc[pl.ds(chunk * CHUNK, CHUNK), :]
        h = jnp.concatenate([h, h], axis=1)[:, :240]
        g3 = readout[0:1, :] + h * (readout[1:2, :] - readout[0:1, :])
        g2 = g3 + dot((g3 * (1.0 - t3 * t3)).astype(BF16), fit3[...], NT)
        g1 = g2 + dot((g2 * (1.0 - t2 * t2)).astype(BF16), fit2[...], NT)
        gd = dot((g1 * (1.0 - f1 * f1)).astype(BF16), fit1[...], NT)
        gd = jnp.concatenate([gd, jnp.zeros((CHUNK, 64), F32)], axis=1)
        parts = [gd[:, g * LANES : (g + 1) * LANES] for g in range(13)]
        for c in range(4):
            left = jnp.concatenate([p * tiled[c] for p in parts], axis=1).astype(BF16)
            left = dot(left, fold[...], NN)
            right = sum(parts[g] * spreads[g][c] for g in range(13))
            for shift in (64, 32, 16):
                right = right + pltpu.roll(right, shift, 1)
            gf = left + jnp.where(lane_m < 16, right, 0.0)
            gfeats[pl.ds(base + c, CHUNK, stride=8), :] = gf * (1.0 / 128.0)
        return carry

    lax.fori_loop(0, lax.div(total + (CHUNK - 1), CHUNK), fit, 0)

    def back(block, carry):
        first = block * BLK
        for b in range(BLK):
            row = order[first + b]
            gf = gfeats[pl.ds(pl.multiple_of((first + b) * 8, 8), 8), :][:, :104]
            qp = dot(gf.astype(BF16), three[first + b], NN)
            at = pl.ds(pl.multiple_of(row * 8, 8), 8)
            qs[at, :] = qp[:, :128]
            ps[at, :] = qp[:, 128:]
        return carry

    lax.fori_loop(0, blocks, back, 0)

    sub = lax.broadcasted_iota(jnp.int32, (LANES, LANES), 0)

    def scatter(s, half):
        base = s * SHARE + half * 8
        at = pl.ds(base, 8)
        idx = nb[s, half * 8 : half * 8 + 8, :]
        off = [geo[n, at, :] for n in range(3)]
        inv, fsw = geo[3, at, :], geo[4, at, :]
        q = [qs[pl.ds(base * 8 + n, 8, stride=8), :] for n in range(4)]
        p = [ps[pl.ds(base * 8 + n, 8, stride=8), :] for n in range(4)]
        inv3 = 0.5 * inv * inv * inv
        strength = fsw * fsw * inv
        qo = q[1] * off[0] + q[2] * off[1] + q[3] * off[2]
        po = p[1] * off[0] + p[2] * off[1] + p[3] * off[2]
        gs = q[0] + inv * qo + strength * (p[0] + inv * po)
        gd2 = -gs * (fsw * inv * 0.125 + fsw * fsw * inv3) - qo * strength * inv3
        si = strength * inv
        g = [jnp.where(idx >= 0, q[1 + c] * si + 2.0 * off[c] * gd2, 0.0) for c in range(3)]
        near = idx < 128
        centre_at = own_row(s, half) == lane8
        grad = jnp.zeros((8, LANES), F32)
        for c in range(3):
            scat[pl.ds(base * 8 + c, 8, stride=8), :] = jnp.where(near, g[c], 0.0)
            scat[pl.ds(base * 8 + 3 + c, 8, stride=8), :] = jnp.where(near, 0.0, g[c])
            total_c = jnp.sum(g[c], axis=1, keepdims=True)
            line = jnp.sum(jnp.where(centre_at, -total_c, 0.0), axis=0, keepdims=True)
            grad = jnp.where(row8 == c, line, grad)
        lhs, rhs = [], []
        for j in range(8):
            lhs.append(scat[pl.ds((base + j) * 8, 8), :].astype(BF16))
            low = nb[s, half * 8 + j : half * 8 + j + 1, :] & 127
            rhs.append(jnp.where(sub == low, 1.0, 0.0).astype(BF16))
        grad = grad + dot(jnp.concatenate(lhs, axis=1), jnp.concatenate(rhs, axis=1), NT)
        if half == 0:
            feats[pl.ds(s * 8, 8), :] = grad
        else:
            feats[pl.ds(s * 8, 8), :] += grad

    for s in range(N_SLAB):
        scatter(s, 0)
    second_half(scatter)
    grads = [feats[pl.ds(s * 8, 8), :] for s in range(N_SLAB)]
    for s in range(N_SLAB):
        edge = jnp.where(lane8 < 64, grads[(s + 1) % N_SLAB], grads[(s - 1) % N_SLAB])
        out[s] = jnp.where(row8 < 3, grads[s], edge)


def force_call(tile, nb, w2t, w3t, cols, fit):
    fit1, b1, fit2, b2, fit3, b3, readout = fit
    _, _, _, _, _, spread, fold = selections()
    rows = N_SLAB * SHARE
    vm = pl.BlockSpec(memory_space=pltpu.VMEM)
    anyw = pl.BlockSpec(memory_space=pl.ANY)
    return pl.pallas_call(
        force_kernel,
        out_shape=jax.ShapeDtypeStruct((N_SLAB, 8, LANES), F32),
        in_specs=[vm] * 6 + [anyw] * 4 + [vm] * 4,
        out_specs=vm,
        scratch_shapes=[
            pltpu.VMEM(((rows + 1) * 8, LANES), F32),
            pltpu.VMEM((5, rows, LANES), F32),
            pltpu.SMEM((rows + 24,), jnp.int32),
            pltpu.SMEM((N_SLAB,), jnp.int32),
            pltpu.VMEM((rows + 8, LANES), F32),
            pltpu.VMEM((rows + 8, 104, 256), BF16),
            pltpu.VMEM(((rows + 8) * 8, LANES), F32),
            pltpu.VMEM(((rows + 8) * 8, LANES), F32),
            pltpu.VMEM(((rows + 1) * 8, LANES), F32),
            pltpu.VMEM(((rows + 1) * 8, LANES), F32),
            pltpu.VMEM((rows * 8, LANES), F32),
            pltpu.VMEM((13 * LANES, LANES), BF16),
            pltpu.VMEM((1600, 240), BF16),
            pltpu.VMEM((240, 240), BF16),
            pltpu.VMEM((240, 240), BF16),
            pltpu.SemaphoreType.DMA((4,)),
        ],
        compiler_params=pltpu.CompilerParams(vmem_limit_bytes=48 << 20),
        name="force",
    )(
        tile, nb, w2t, w3t, cols, jnp.asarray(spread), jnp.asarray(fold, BF16),
        fit1, fit2, fit3, b1[None], b2[None], b3[None], readout,
    )


def prepare_kernel(pos, types, halo, scale, shift, w2, b2, w3, b3, s1, a2, p1, a3, p2, tile, w2t, w3t, cols):
    tile[...] = own_tile(pos[...], types[...], halo[...])
    prepare_weights(scale, shift, w2, b2, w3, b3, s1, a2, p1, a3, p2, w2t, w3t, cols)


def kick_kernel(msgs, vel, types, halo, forces, kicked):
    got = msgs[0]
    for s in range(1, N_SLAB):
        got = got + msgs[s]
    bins = pltpu.roll(spread_rows(halo[...], 8), 64, 1)[0:1]
    hit = jnp.where(lax.broadcasted_iota(jnp.int32, (LANES, LANES), 0) == bins, 1.0, 0.0)
    back = lax.dot_general(got, hit, NT, preferred_element_type=F32, precision=HIGH)
    force = -(got[0:3] + back[3:6])
    forces[...] = force
    kicked[...] = vel[...] + STEP * jnp.where(types[...] == 1, 1.0, 1.0 / HEAVY) * force


def local(
    positions, velocities, atom_types, live_atoms, halo_rows, neighbours,
    type_scale, type_shift, embed_two, embed_bias_two, embed_three, embed_bias_three,
    fit_first, fit_bias_first, fit_second, fit_bias_second, fit_third, fit_bias_third, fit_readout,
):
    del live_atoms
    pos, vel, types = positions[:, 0, :], velocities[:, 0, :], atom_types[None]
    s1, a2, p1, a3, p2, _, _ = selections()
    tile, w2t, w3t, cols = pl.pallas_call(
        prepare_kernel,
        out_shape=(
            jax.ShapeDtypeStruct((8, LANES), F32),
            jax.ShapeDtypeStruct((56, 32), BF16),
            jax.ShapeDtypeStruct((104, 56), BF16),
            jax.ShapeDtypeStruct((4, 32, LANES), F32),
        ),
        name="prepare",
    )(
        pos, types, halo_rows, type_scale, type_shift, embed_two, embed_bias_two[None],
        embed_three, embed_bias_three[None], jnp.asarray(s1), jnp.asarray(a2, BF16),
        jnp.asarray(p1, BF16), jnp.asarray(a3, BF16), jnp.asarray(p2, BF16),
    )
    me = lax.axis_index("slab")
    dealt = jnp.moveaxis(neighbours.reshape(SHARE, N_SLAB, LANES), 1, 0).astype(F32)
    dealt = jnp.roll(dealt, me, axis=0)
    parcel = jnp.concatenate([jnp.broadcast_to(tile, (N_SLAB, 8, LANES)), dealt], axis=1)
    parcel = lax.all_to_all(parcel, "slab", 0, 0, tiled=True)
    nb = parcel[:, 8:].astype(jnp.int32)
    msgs = force_call(
        parcel[:, :8], nb, w2t, w3t, cols,
        (fit_first, fit_bias_first, fit_second, fit_bias_second, fit_third, fit_bias_third, fit_readout),
    )
    msgs = lax.all_to_all(msgs, "slab", 0, 0, tiled=True)
    forces, kicked = pl.pallas_call(
        kick_kernel,
        out_shape=(jax.ShapeDtypeStruct((3, LANES), F32),) * 2,
        name="kick",
    )(msgs, vel, types, halo_rows)
    own = lax.axis_index("bead")
    cos, travel, spring = (jnp.asarray(m) for m in mode_matrices())
    col = lambda m: lax.dynamic_index_in_dim(m, own, 1, keepdims=False)[:BEADS_HERE, None, None]
    mixed = jnp.stack(
        [
            col(cos) * pos + col(travel) * kicked,
            col(-spring) * pos + col(cos) * kicked,
        ],
        axis=1,
    )
    mixed = lax.all_to_all(mixed, "bead", 0, 0, tiled=True).sum(axis=0)
    return mixed[0][:, None, :], mixed[1][:, None, :], forces[:, None, :]


BEADS_HERE = BEADS


def solution(mesh):
    wide = P(None, "bead", "slab")
    return jax.shard_map(
        local,
        mesh=mesh,
        in_specs=(wide, wide, P("slab"), P("slab"), P("slab", None), P("slab", None)) + (P(),) * 13,
        out_specs=(wide, wide, wide),
        check_vma=False,
    )
```

```python
import functools

import jax
import jax.numpy as jnp
import numpy as np
from jax import lax
from jax.experimental import pallas as pl
from jax.experimental.pallas import tpu as pltpu
from jax.sharding import PartitionSpec as P

BEADS = 64
N_SLAB = 8
SHARE = 16
LANES = 128
STEP = 0.25
HEAVY = 16.0
BLK = 8
CHUNK = 64
F32 = jnp.float32
BF16 = jnp.bfloat16
NT = (((1,), (1,)), ((), ()))
HIGH = lax.Precision.HIGHEST


def two_feature(row):
    if row < 24:
        return row
    if row < 48:
        return row + 1
    if row < 52:
        return (24, 49)[(row - 48) % 2]
    return -1


def three_feature(row):
    if row < 48:
        return two_feature(row)
    if row < 96:
        return 50 + two_feature(row - 48)
    if row < 100:
        return (24, 49, 74, 99)[row - 96]
    return -1


def selections():
    one_of = [k if k < 24 else 24 if k < 28 else -1 for k in range(32)]
    s1 = np.zeros((32, 25), np.float32)
    for k, f in enumerate(one_of):
        if f >= 0:
            s1[k, f] = 1
    a2 = np.zeros((56, 50), np.float32)
    for k in range(56):
        if two_feature(k) >= 0:
            a2[k, two_feature(k)] = 1
    b1 = np.zeros((25, 32), np.float32)
    for f in range(25):
        b1[f, f] = 1
    a3 = np.zeros((104, 100), np.float32)
    where = np.zeros((104,), np.int32)
    where[100:] = 127
    for k in range(104):
        if three_feature(k) >= 0:
            a3[k, three_feature(k)] = 1
            where[three_feature(k)] = k
    b2 = np.zeros((50, 56), np.float32)
    for k in range(50):
        b2[two_feature(k), k] = 1
    spread = np.full((16, LANES), 127, np.int32)
    fold = np.zeros((13 * LANES, LANES), np.float32)
    for g in range(13):
        for lane in range(LANES):
            e = 8 * g + lane // 16
            spread[g, lane] = where[e]
            if e < 100:
                fold[g * LANES + lane, where[e]] = 1
    return s1, a2, b1, a3, b2, spread, fold


def mode_matrices():
    n = BEADS
    j, k = np.arange(n)[:, None], np.arange(n)[None, :]
    angle = 2 * np.pi * ((j * k) % n) / n
    basis = np.where(
        k == 0,
        1 / np.sqrt(n),
        np.where(
            k < n // 2,
            np.sqrt(2 / n) * np.cos(angle),
            np.where(k == n // 2, np.where(j % 2 == 0, 1.0, -1.0) / np.sqrt(n), np.sqrt(2 / n) * np.sin(angle)),
        ),
    )
    sine = np.sin(np.pi * np.arange(n) / n)
    ratio = 2 * sine
    theta = 1.2 * n * sine
    travel = np.where(np.arange(n) == 0, 1.0, np.sin(theta) / np.where(np.arange(n) == 0, 1.0, ratio))
    return tuple(
        ((basis * d[None, :]) @ basis.T).astype(np.float32)
        for d in (np.cos(theta), travel, ratio * np.sin(theta))
    )


def lanes_of(table, index):
    return jnp.take_along_axis(table, index, axis=1, mode="promise_in_bounds")


def spread_rows(row, count):
    return jnp.broadcast_to(row, (count, row.shape[1]))


def own_tile(pos, types, halo):
    hydrogen = jnp.where(types == 1, 1.0, 0.0).astype(F32)
    mine = jnp.concatenate([pos, hydrogen], axis=0)
    wide = jnp.concatenate([mine, mine], axis=0)
    sent = lanes_of(wide, spread_rows(halo, 8))
    return jnp.where(lax.broadcasted_iota(jnp.int32, (8, LANES), 0) < 4, wide, sent)


def thirds(row):
    high = row.astype(BF16).astype(F32)
    rest = row - high
    mid = rest.astype(BF16).astype(F32)
    return high, mid, rest - mid


def bias_rows(bias, first, count):
    high, mid, low = thirds(bias)
    at = lax.broadcasted_iota(jnp.int32, (count, bias.shape[1]), 0)
    return jnp.where(at == first, high, jnp.where(at == first + 1, mid, jnp.where(at == first + 2, low, 0.0)))


def prepare_weights(scale, shift, w2, b2, w3, b3, s1, a2, p1, a3, p2, w2t, w3t, cols):
    dot = functools.partial(lax.dot_general, preferred_element_type=F32)
    two = dot(a2[...], w2[...], NT).astype(BF16)
    two = dot(two, p1[...], (((1,), (0,)), ((), ())))
    two = two + dot(a2[...], bias_rows(b2[...], 28, 32).astype(BF16), NT)
    w2t[...] = two.astype(BF16)
    three = dot(a3[...], w3[...], NT).astype(BF16)
    three = dot(three, p2[...], (((1,), (0,)), ((), ())))
    three = three + dot(a3[...], bias_rows(b3[...], 52, 56).astype(BF16), NT)
    w3t[...] = three.astype(BF16)
    at = lax.broadcasted_iota(jnp.int32, (32, LANES), 0)
    ones = jnp.where((at >= 28) & (at < 31), 20.0, 0.0)
    for kind in range(2):
        for n, ref in enumerate((scale, shift)):
            col = dot(s1[...], spread_rows(ref[kind : kind + 1, :], LANES), NT, precision=HIGH)
            cols[2 * n + kind] = col + ones if n else col


def force_kernel(
    tile, nb, w2t, w3t, cols, spread, fold_hbm, fit1_hbm, fit2_hbm, fit3_hbm, c1, c2, c3, readout,
    out,
    env, geo, order, count, hc, three, feats, gfeats, qs, ps, scat, fold, fit1, fit2, fit3, sems,
):
    me = lax.axis_index("slab")
    loads = [
        pltpu.make_async_copy(src, dst, sems.at[n])
        for n, (src, dst) in enumerate(
            ((fit1_hbm, fit1), (fit2_hbm, fit2), (fit3_hbm, fit3), (fold_hbm, fold))
        )
    ]
    for load in loads:
        load.start()
    dot = functools.partial(lax.dot_general, preferred_element_type=F32)
    NN = (((1,), (0,)), ((), ()))
    lane8 = lax.broadcasted_iota(jnp.int32, (8, LANES), 1)
    row8 = lax.broadcasted_iota(jnp.int32, (8, LANES), 0)

    for s in range(N_SLAB):
        count[s] = jnp.sum(jnp.where(nb[s][:, 0:1] >= 0, 1.0, 0.0)).astype(jnp.int32)
    total = jnp.int32(0)
    for s in range(N_SLAB):
        for j in range(SHARE):
            order[total + j] = s * SHARE + j
        total = total + count[s]
    for j in range(BLK):
        order[total + j] = N_SLAB * SHARE
    env[pl.ds(N_SLAB * SHARE * 8, 8), :] = jnp.zeros((8, LANES), F32)

    def own_row(s, half):
        return (row8 + half * 8) * 8 + lax.rem(me - s + N_SLAB, N_SLAB)

    def geometry(s, half):
        before = lax.rem(s + N_SLAB - 1, N_SLAB)
        after = lax.rem(s + 1, N_SLAB)
        idx = nb[s, half * 8 : half * 8 + 8, :]
        low = idx & 127
        far = idx >= 128
        own = tile[s]
        edge = pltpu.roll(jnp.where(lane8 >= 64, tile[before], tile[after]), 64, 1)
        centre_at = own_row(s, half)
        base = s * SHARE + half * 8
        got = []
        for c in range(4):
            near = lanes_of(spread_rows(own[c : c + 1], 8), low)
            there = lanes_of(spread_rows(edge[4 + c : 5 + c], 8), low)
            got.append(jnp.where(far, there, near))
        mid = [lanes_of(spread_rows(own[c : c + 1], 8), centre_at) for c in range(4)]
        off = [got[c] - mid[c] for c in range(3)]
        d2 = off[0] * off[0] + off[1] * off[1] + off[2] * off[2]
        inv = lax.rsqrt(d2 + 0.25)
        fsw = jnp.where(idx >= 0, jnp.maximum(1.0 - d2 * (1.0 / 16.0), 0.0), 0.0)
        strength = fsw * fsw * inv
        si = strength * inv
        at = pl.ds(base, 8)
        for n, value in enumerate((*off, inv, fsw)):
            geo[n, at, :] = value
        for n, value in enumerate((strength, si * off[0], si * off[1], si * off[2], got[3], mid[3])):
            env[pl.ds(base * 8 + n, 8, stride=8), :] = value

    for s in range(N_SLAB):
        geometry(s, 0)

    def second_half(fn):
        def step(s, carry):
            @pl.when(count[s] > 8)
            def _():
                fn(s, 1)
            return carry

        lax.fori_loop(0, N_SLAB, step, 0)

    second_half(geometry)

    sc0, sc1, sh0, sh1 = 0, 1, 2, 3

    def forward(block, carry):
        first = block * BLK
        e, one, done = [], [], []
        for b in range(BLK):
            row = order[first + b]
            v = env[pl.ds(pl.multiple_of(row * 8, 8), 8), :]
            e.append(v)
            hyd = v[4:5] > 0.5
            sc = jnp.where(hyd, cols[sc1], cols[sc0])
            t = jnp.tanh(v[0:1] * sc + jnp.where(hyd, cols[sh1], cols[sh0]))
            one.append((t, (1.0 - t * t) * sc))
            hc[pl.ds(first + b, 1), :] = v[5:6]
        x = jnp.concatenate([a.astype(BF16) for pair in one for a in pair], axis=1)
        z = dot(w2t[...], x, NN)
        two = []
        for b in range(BLK):
            t1, d1 = one[b]
            t = jnp.tanh(z[:, 256 * b : 256 * b + 128])
            d = (1.0 - t * t) * z[:, 256 * b + 128 : 256 * b + 256]
            two.append((
                t + jnp.concatenate([t1[:24], t1[:24], t1[24:]], axis=0),
                d + jnp.concatenate([d1[:24], d1[:24], d1[24:]], axis=0),
            ))
        x = jnp.concatenate([a.astype(BF16) for pair in two for a in pair], axis=1)
        z = dot(w3t[...], x, NN)
        for b in range(BLK):
            t2, d2 = two[b]
            t = jnp.tanh(z[:, 256 * b : 256 * b + 128])
            d = (1.0 - t * t) * z[:, 256 * b + 128 : 256 * b + 256]
            l3 = (t + jnp.concatenate([t2[:48], t2[:48], t2[48:]], axis=0)).astype(BF16)
            d3 = (d + jnp.concatenate([d2[:48], d2[:48], d2[48:]], axis=0)).astype(BF16)
            three[first + b] = jnp.concatenate([l3, d3], axis=1)
            f = dot(e[b].astype(BF16), l3, NT) * (1.0 / 128.0)
            feats[pl.ds(pl.multiple_of((first + b) * 8, 8), 8), :] = jnp.concatenate(
                [f, jnp.zeros((8, 24), F32)], axis=1
            )
        return carry

    blocks = lax.div(total + (BLK - 1), BLK)
    lax.fori_loop(0, blocks, forward, 0)

    for load in loads:
        load.wait()

    lane_m = lax.broadcasted_iota(jnp.int32, (CHUNK, LANES), 1)

    def fit(chunk, carry):
        base = chunk * (CHUNK * 8)
        fs = [feats[pl.ds(base + c, CHUNK, stride=8), :] for c in range(4)]
        tiled = [lanes_of(f, lane_m & 15) for f in fs]
        spreads = [
            [lanes_of(f, spread_rows(spread[g : g + 1, :], CHUNK)) for f in fs] for g in range(13)
        ]
        desc = [sum(spreads[g][c] * tiled[c] for c in range(4)) for g in range(13)]
        desc = jnp.concatenate(desc, axis=1).astype(BF16)[:, :1600]
        f1 = jnp.tanh(dot(desc, fit1[...], NN) + c1[...])
        t2 = jnp.tanh(dot(f1.astype(BF16), fit2[...], NN) + c2[...])
        f2 = t2 + f1
        t3 = jnp.tanh(dot(f2.astype(BF16), fit3[...], NN) + c3[...])
        h = hc[pl.ds(chunk * CHUNK, CHUNK), :]
        h = jnp.concatenate([h, h], axis=1)[:, :240]
        g3 = readout[0:1, :] + h * (readout[1:2, :] - readout[0:1, :])
        g2 = g3 + dot((g3 * (1.0 - t3 * t3)).astype(BF16), fit3[...], NT)
        g1 = g2 + dot((g2 * (1.0 - t2 * t2)).astype(BF16), fit2[...], NT)
        gd = dot((g1 * (1.0 - f1 * f1)).astype(BF16), fit1[...], NT)
        gd = jnp.concatenate([gd, jnp.zeros((CHUNK, 64), F32)], axis=1)
        parts = [gd[:, g * LANES : (g + 1) * LANES] for g in range(13)]
        for c in range(4):
            left = jnp.concatenate([p * tiled[c] for p in parts], axis=1).astype(BF16)
            left = dot(left, fold[...], NN)
            right = sum(parts[g] * spreads[g][c] for g in range(13))
            for shift in (64, 32, 16):
                right = right + pltpu.roll(right, shift, 1)
            gf = left + jnp.where(lane_m < 16, right, 0.0)
            gfeats[pl.ds(base + c, CHUNK, stride=8), :] = gf * (1.0 / 128.0)
        return carry

    lax.fori_loop(0, lax.div(total + (CHUNK - 1), CHUNK), fit, 0)

    def back(block, carry):
        first = block * BLK
        for b in range(BLK):
            row = order[first + b]
            gf = gfeats[pl.ds(pl.multiple_of((first + b) * 8, 8), 8), :][:, :104]
            qp = dot(gf.astype(BF16), three[first + b], NN)
            at = pl.ds(pl.multiple_of(row * 8, 8), 8)
            qs[at, :] = qp[:, :128]
            ps[at, :] = qp[:, 128:]
        return carry

    lax.fori_loop(0, blocks, back, 0)

    sub = lax.broadcasted_iota(jnp.int32, (LANES, LANES), 0)

    def scatter(s, half):
        base = s * SHARE + half * 8
        at = pl.ds(base, 8)
        idx = nb[s, half * 8 : half * 8 + 8, :]
        off = [geo[n, at, :] for n in range(3)]
        inv, fsw = geo[3, at, :], geo[4, at, :]
        q = [qs[pl.ds(base * 8 + n, 8, stride=8), :] for n in range(4)]
        p = [ps[pl.ds(base * 8 + n, 8, stride=8), :] for n in range(4)]
        inv3 = 0.5 * inv * inv * inv
        strength = fsw * fsw * inv
        qo = q[1] * off[0] + q[2] * off[1] + q[3] * off[2]
        po = p[1] * off[0] + p[2] * off[1] + p[3] * off[2]
        gs = q[0] + inv * qo + strength * (p[0] + inv * po)
        gd2 = -gs * (fsw * inv * 0.125 + fsw * fsw * inv3) - qo * strength * inv3
        si = strength * inv
        g = [jnp.where(idx >= 0, q[1 + c] * si + 2.0 * off[c] * gd2, 0.0) for c in range(3)]
        near = idx < 128
        centre_at = own_row(s, half) == lane8
        grad = jnp.zeros((8, LANES), F32)
        for c in range(3):
            scat[pl.ds(base * 8 + c, 8, stride=8), :] = jnp.where(near, g[c], 0.0)
            scat[pl.ds(base * 8 + 3 + c, 8, stride=8), :] = jnp.where(near, 0.0, g[c])
            total_c = jnp.sum(g[c], axis=1, keepdims=True)
            line = jnp.sum(jnp.where(centre_at, -total_c, 0.0), axis=0, keepdims=True)
            grad = jnp.where(row8 == c, line, grad)
        lhs, rhs = [], []
        for j in range(8):
            lhs.append(scat[pl.ds((base + j) * 8, 8), :].astype(BF16))
            low = nb[s, half * 8 + j : half * 8 + j + 1, :] & 127
            rhs.append(jnp.where(sub == low, 1.0, 0.0).astype(BF16))
        grad = grad + dot(jnp.concatenate(lhs, axis=1), jnp.concatenate(rhs, axis=1), NT)
        if half == 0:
            feats[pl.ds(s * 8, 8), :] = grad
        else:
            feats[pl.ds(s * 8, 8), :] += grad

    for s in range(N_SLAB):
        scatter(s, 0)
    second_half(scatter)
    grads = [feats[pl.ds(s * 8, 8), :] for s in range(N_SLAB)]
    for s in range(N_SLAB):
        edge = jnp.where(lane8 < 64, grads[(s + 1) % N_SLAB], grads[(s - 1) % N_SLAB])
        out[s] = jnp.where(row8 < 3, grads[s], edge)


def force_call(tile, nb, w2t, w3t, cols, fit):
    fit1, b1, fit2, b2, fit3, b3, readout = fit
    _, _, _, _, _, spread, fold = selections()
    rows = N_SLAB * SHARE
    vm = pl.BlockSpec(memory_space=pltpu.VMEM)
    anyw = pl.BlockSpec(memory_space=pl.ANY)
    return pl.pallas_call(
        force_kernel,
        out_shape=jax.ShapeDtypeStruct((N_SLAB, 8, LANES), F32),
        in_specs=[vm] * 6 + [anyw] * 4 + [vm] * 4,
        out_specs=vm,
        scratch_shapes=[
            pltpu.VMEM(((rows + 1) * 8, LANES), F32),
            pltpu.VMEM((5, rows, LANES), F32),
            pltpu.SMEM((rows + 24,), jnp.int32),
            pltpu.SMEM((N_SLAB,), jnp.int32),
            pltpu.VMEM((rows + 8, LANES), F32),
            pltpu.VMEM((rows + 8, 104, 256), BF16),
            pltpu.VMEM(((rows + 8) * 8, LANES), F32),
            pltpu.VMEM(((rows + 8) * 8, LANES), F32),
            pltpu.VMEM(((rows + 1) * 8, LANES), F32),
            pltpu.VMEM(((rows + 1) * 8, LANES), F32),
            pltpu.VMEM((rows * 8, LANES), F32),
            pltpu.VMEM((13 * LANES, LANES), BF16),
            pltpu.VMEM((1600, 240), BF16),
            pltpu.VMEM((240, 240), BF16),
            pltpu.VMEM((240, 240), BF16),
            pltpu.SemaphoreType.DMA((4,)),
        ],
        compiler_params=pltpu.CompilerParams(vmem_limit_bytes=48 << 20),
        name="force",
    )(
        tile, nb, w2t, w3t, cols, jnp.asarray(spread), jnp.asarray(fold, BF16),
        fit1, fit2, fit3, b1[None], b2[None], b3[None], readout,
    )


MESH = pl.DeviceIdType.MESH
NZ = 16
NY = 4
REACH = 4


def greet(peers):
    barrier = pltpu.get_barrier_semaphore()
    for peer in peers:
        pl.semaphore_signal(barrier, inc=1, device_id=peer, device_id_type=MESH)
    pl.semaphore_wait(barrier, len(peers))


def send(src, dst, out_sem, in_sem, peer):
    copy = pltpu.make_async_remote_copy(
        src_ref=src, dst_ref=dst, send_sem=out_sem, recv_sem=in_sem, device_id=peer, device_id_type=MESH
    )
    copy.start()
    return copy


def slab_peers():
    me = lax.axis_index("slab")
    return me, [{"slab": lax.rem(me + i, N_SLAB)} for i in range(1, N_SLAB)]


def exchange_kernel(
    pos, types, halo, lists, scale, shift, w2, b2, w3, b3, s1, a2, p1, a3, p2,
    tiles, nb, w2t, w3t, cols,
    tile_out, tile_in, list_out, list_in, own_sem,
):
    me, peers = slab_peers()
    tiles[me] = own_tile(pos[...], types[...], halo[...])
    greet(peers)
    copies = []
    for i, peer in enumerate(peers):
        copies.append(send(lists.at[:, i + 1, :], nb.at[me], list_out.at[i], list_in.at[i], peer))
    for i, peer in enumerate(peers):
        copies.append(send(tiles.at[me], tiles.at[me], tile_out.at[i], tile_in.at[i], peer))
    own = pltpu.make_async_copy(lists.at[:, 0, :], nb.at[me], own_sem)
    own.start()
    prepare_weights(scale, shift, w2, b2, w3, b3, s1, a2, p1, a3, p2, w2t, w3t, cols)
    own.wait()
    for copy in copies:
        copy.wait()


def finish_kernel(
    msgs, pos, vel, types, halo, coefs,
    pos_out, vel_out, force_out,
    inbox, ring, mixed, ybox, slab_out, slab_in, ring_out, ring_in, far_out, far_in, y_out, y_in,
):
    me, peers = slab_peers()
    bead = lax.axis_index("bead")
    z, y = lax.div(bead, NY), lax.rem(bead, NY)

    def along(d):
        return {"bead": lax.rem(z + NZ + d, NZ) * NY + y}

    steps = [d for k in range(1, REACH + 1) for d in (k, -k)]
    yet = [lax.rem(y + k, NY) for k in range(1, NY)]
    ypeers = [{"bead": z * NY + other} for other in yet]
    greet(peers + [along(d) for d in steps] + ypeers)

    copies = [
        send(msgs.at[lax.rem(me + i + 1, N_SLAB)], inbox.at[i], slab_out.at[i], slab_in.at[i], peer)
        for i, peer in enumerate(peers)
    ]
    bins = pltpu.roll(spread_rows(halo[...], 8), 64, 1)[0:1]
    hit = jnp.where(lax.broadcasted_iota(jnp.int32, (LANES, LANES), 0) == bins, 1.0, 0.0)
    got = msgs[me]
    for i, copy in enumerate(copies):
        copy.wait()
        got = got + inbox[i]
    back = lax.dot_general(got, hit, NT, preferred_element_type=F32, precision=HIGH)
    force = -(got[0:3] + back[3:6])
    kicked = vel[...] + STEP * jnp.where(types[...] == 1, 1.0, 1.0 / HEAVY) * force
    own = ring.at[8]
    own[...] = jnp.concatenate([pos[...], kicked, jnp.zeros((2, LANES), F32)], axis=0)

    near = {
        d: send(own, ring.at[8 - d], ring_out.at[n], ring_in.at[n], along(d)) for n, d in enumerate(steps)
    }
    force_out[...] = force
    for d in steps:
        if d > 0:
            near[d].wait_recv()
    up = send(ring.at[pl.ds(4, 4)], ring.at[pl.ds(0, 4)], far_out.at[0], far_in.at[0], along(REACH))
    for d in steps:
        if d < 0:
            near[d].wait_recv()
    down = send(ring.at[pl.ds(9, 3)], ring.at[pl.ds(13, 3)], far_out.at[1], far_in.at[1], along(-REACH))
    for d in steps:
        near[d].wait_send()
    up.wait()
    down.wait()

    blocks = jnp.concatenate([ring[n] for n in range(NZ)], axis=0)
    sums = lax.dot_general(
        coefs[y], blocks, (((1,), (0,)), ((), ())), preferred_element_type=F32, precision=HIGH
    )
    for k in range(NY):
        mixed[k] = sums[8 * k : 8 * k + 8]
    copies = [
        send(mixed.at[other], ybox.at[i], y_out.at[i], y_in.at[i], peer)
        for i, (other, peer) in enumerate(zip(yet, ypeers))
    ]
    done = mixed[y]
    for i, copy in enumerate(copies):
        copy.wait()
        done = done + ybox[i]
    pos_out[...] = done[0:3]
    vel_out[...] = done[3:6]


def ring_coefficients():
    cos, travel, spring = (m[:, 0].astype(np.float64) for m in mode_matrices())
    table = np.zeros((NY, NY, 8, NZ, 8), np.float32)
    for y in range(NY):
        for to in range(NY):
            for slot in range(NZ):
                apart = (to - y - NY * (slot - 8)) % BEADS
                for c in range(3):
                    table[y, to, c, slot, c] = cos[apart]
                    table[y, to, c, slot, 3 + c] = travel[apart]
                    table[y, to, 3 + c, slot, c] = -spring[apart]
                    table[y, to, 3 + c, slot, 3 + c] = cos[apart]
    return table.reshape(NY, NY * 8, NZ * 8)


def finish_call(msgs, pos, vel, types, halo):
    dma = lambda n: pltpu.SemaphoreType.DMA((n,))
    near = 2 * REACH
    return pl.pallas_call(
        finish_kernel,
        out_shape=(jax.ShapeDtypeStruct((3, LANES), F32),) * 3,
        scratch_shapes=[
            pltpu.VMEM((7, 8, LANES), F32),
            pltpu.VMEM((NZ, 8, LANES), F32),
            pltpu.VMEM((NY, 8, LANES), F32),
            pltpu.VMEM((NY - 1, 8, LANES), F32),
            dma(7), dma(7), dma(near), dma(near), dma(2), dma(2), dma(NY - 1), dma(NY - 1),
        ],
        compiler_params=pltpu.CompilerParams(collective_id=1, has_side_effects=True),
        name="finish",
    )(msgs, pos, vel, types, halo, jnp.asarray(ring_coefficients()))


def local(
    positions, velocities, atom_types, live_atoms, halo_rows, neighbours,
    type_scale, type_shift, embed_two, embed_bias_two, embed_three, embed_bias_three,
    fit_first, fit_bias_first, fit_second, fit_bias_second, fit_third, fit_bias_third, fit_readout,
):
    del live_atoms
    pos, vel, types = positions[:, 0, :], velocities[:, 0, :], atom_types[None]
    s1, a2, p1, a3, p2, _, _ = selections()
    dma = lambda n: pltpu.SemaphoreType.DMA((n,))
    vm = pl.BlockSpec(memory_space=pltpu.VMEM)
    tiles, nb, w2t, w3t, cols = pl.pallas_call(
        exchange_kernel,
        out_shape=(
            jax.ShapeDtypeStruct((N_SLAB, 8, LANES), F32),
            jax.ShapeDtypeStruct((N_SLAB, SHARE, LANES), jnp.int32),
            jax.ShapeDtypeStruct((56, 32), BF16),
            jax.ShapeDtypeStruct((104, 56), BF16),
            jax.ShapeDtypeStruct((4, 32, LANES), F32),
        ),
        in_specs=[vm] * 3 + [pl.BlockSpec(memory_space=pl.ANY)] + [vm] * 11,
        out_specs=(vm,) * 5,
        scratch_shapes=[dma(7), dma(7), dma(7), dma(7), pltpu.SemaphoreType.DMA],
        compiler_params=pltpu.CompilerParams(collective_id=0, has_side_effects=True),
        name="exchange",
    )(
        pos, types, halo_rows, neighbours.reshape(SHARE, N_SLAB, LANES), type_scale, type_shift,
        embed_two, embed_bias_two[None], embed_three, embed_bias_three[None], jnp.asarray(s1),
        jnp.asarray(a2, BF16), jnp.asarray(p1, BF16), jnp.asarray(a3, BF16), jnp.asarray(p2, BF16),
    )
    msgs = force_call(
        tiles, nb, w2t, w3t, cols,
        (fit_first, fit_bias_first, fit_second, fit_bias_second, fit_third, fit_bias_third, fit_readout),
    )
    outs = finish_call(msgs, pos, vel, types, halo_rows)
    return tuple(out[:, None, :] for out in outs)


def solution(mesh):
    wide = P(None, "bead", "slab")
    return jax.shard_map(
        local,
        mesh=mesh,
        in_specs=(wide, wide, P("slab"), P("slab"), P("slab", None), P("slab", None)) + (P(),) * 13,
        out_specs=(wide, wide, wide),
        check_vma=False,
    )
```

```python
import functools

import jax
import jax.numpy as jnp
import numpy as np
from jax import lax
from jax.experimental import pallas as pl
from jax.experimental.pallas import tpu as pltpu
from jax.sharding import PartitionSpec as P

BEADS = 64
N_SLAB = 8
SHARE = 16
LANES = 128
STEP = 0.25
HEAVY = 16.0
BLK = 8
CHUNK = 64
F32 = jnp.float32
BF16 = jnp.bfloat16
NT = (((1,), (1,)), ((), ()))
HIGH = lax.Precision.HIGHEST
PLACE = pltpu.HBM


def two_feature(row):
    if row < 24:
        return row
    if row < 48:
        return row + 1
    if row < 52:
        return (24, 49)[(row - 48) % 2]
    return -1


def three_feature(row):
    if row < 48:
        return two_feature(row)
    if row < 96:
        return 50 + two_feature(row - 48)
    if row < 100:
        return (24, 49, 74, 99)[row - 96]
    return -1


def selections():
    one_of = [k if k < 24 else 24 if k < 28 else -1 for k in range(32)]
    s1 = np.zeros((32, 25), np.float32)
    for k, f in enumerate(one_of):
        if f >= 0:
            s1[k, f] = 1
    a2 = np.zeros((56, 50), np.float32)
    for k in range(56):
        if two_feature(k) >= 0:
            a2[k, two_feature(k)] = 1
    b1 = np.zeros((25, 32), np.float32)
    for f in range(25):
        b1[f, f] = 1
    a3 = np.zeros((104, 100), np.float32)
    where = np.zeros((104,), np.int32)
    where[100:] = 127
    for k in range(104):
        if three_feature(k) >= 0:
            a3[k, three_feature(k)] = 1
            where[three_feature(k)] = k
    b2 = np.zeros((50, 56), np.float32)
    for k in range(50):
        b2[two_feature(k), k] = 1
    spread = np.full((16, LANES), 127, np.int32)
    fold = np.zeros((13 * LANES, LANES), np.float32)
    for g in range(13):
        for lane in range(LANES):
            e = 8 * g + lane // 16
            spread[g, lane] = where[e]
            if e < 100:
                fold[g * LANES + lane, where[e]] = 1
    return s1, a2, b1, a3, b2, spread, fold


def mode_matrices():
    n = BEADS
    j, k = np.arange(n)[:, None], np.arange(n)[None, :]
    angle = 2 * np.pi * ((j * k) % n) / n
    basis = np.where(
        k == 0,
        1 / np.sqrt(n),
        np.where(
            k < n // 2,
            np.sqrt(2 / n) * np.cos(angle),
            np.where(k == n // 2, np.where(j % 2 == 0, 1.0, -1.0) / np.sqrt(n), np.sqrt(2 / n) * np.sin(angle)),
        ),
    )
    sine = np.sin(np.pi * np.arange(n) / n)
    ratio = 2 * sine
    theta = 1.2 * n * sine
    travel = np.where(np.arange(n) == 0, 1.0, np.sin(theta) / np.where(np.arange(n) == 0, 1.0, ratio))
    return tuple(
        ((basis * d[None, :]) @ basis.T).astype(np.float32)
        for d in (np.cos(theta), travel, ratio * np.sin(theta))
    )


def lanes_of(table, index):
    return jnp.take_along_axis(table, index, axis=1, mode="promise_in_bounds")


def spread_rows(row, count):
    return jnp.broadcast_to(row, (count, row.shape[1]))


def own_tile(pos, types, halo):
    hydrogen = jnp.where(types == 1, 1.0, 0.0).astype(F32)
    mine = jnp.concatenate([pos, hydrogen], axis=0)
    wide = jnp.concatenate([mine, mine], axis=0)
    sent = lanes_of(wide, spread_rows(halo, 8))
    return jnp.where(lax.broadcasted_iota(jnp.int32, (8, LANES), 0) < 4, wide, sent)


def thirds(row):
    high = row.astype(BF16).astype(F32)
    rest = row - high
    mid = rest.astype(BF16).astype(F32)
    return high, mid, rest - mid


def bias_rows(bias, first, count):
    high, mid, low = thirds(bias)
    at = lax.broadcasted_iota(jnp.int32, (count, bias.shape[1]), 0)
    return jnp.where(at == first, high, jnp.where(at == first + 1, mid, jnp.where(at == first + 2, low, 0.0)))


def prepare_weights(scale, shift, w2, b2, w3, b3, s1, a2, p1, a3, p2, w2t, w3t, cols):
    dot = functools.partial(lax.dot_general, preferred_element_type=F32)
    two = dot(a2[...], w2[...], NT).astype(BF16)
    two = dot(two, p1[...], (((1,), (0,)), ((), ())))
    two = two + dot(a2[...], bias_rows(b2[...], 28, 32).astype(BF16), NT)
    w2t[...] = two.astype(BF16)
    three = dot(a3[...], w3[...], NT).astype(BF16)
    three = dot(three, p2[...], (((1,), (0,)), ((), ())))
    three = three + dot(a3[...], bias_rows(b3[...], 52, 56).astype(BF16), NT)
    w3t[...] = three.astype(BF16)
    at = lax.broadcasted_iota(jnp.int32, (32, LANES), 0)
    ones = jnp.where((at >= 28) & (at < 31), 20.0, 0.0)
    for kind in range(2):
        for n, ref in enumerate((scale, shift)):
            col = dot(s1[...], spread_rows(ref[kind : kind + 1, :], LANES), NT, precision=HIGH)
            cols[2 * n + kind] = col + ones if n else col


def fetch(pairs, sems, first=0):
    loads = [pltpu.make_async_copy(src, dst, sems.at[first + n]) for n, (src, dst) in enumerate(pairs)]
    for load in loads:
        load.start()
    return loads


def force_kernel(*refs):
    given, out, held, rest = refs[:14], refs[14], refs[15:29], refs[29:]
    (
        tile, nb, w2t, w3t, cols, spread, c1, c2, c3, readout, fit1, fit2, fit3, fold,
    ) = held
    env, geo, order, count, hc, three, feats, gfeats, qs, ps, scat, sems = rest
    me = lax.axis_index("slab")
    loads = fetch(list(zip(given, held)), sems)
    for load in loads[:2]:
        load.wait()
    dot = functools.partial(lax.dot_general, preferred_element_type=F32)
    NN = (((1,), (0,)), ((), ()))
    lane8 = lax.broadcasted_iota(jnp.int32, (8, LANES), 1)
    row8 = lax.broadcasted_iota(jnp.int32, (8, LANES), 0)

    for s in range(N_SLAB):
        count[s] = jnp.sum(jnp.where(nb[s][:, 0:1] >= 0, 1.0, 0.0)).astype(jnp.int32)
    total = jnp.int32(0)
    for s in range(N_SLAB):
        for j in range(SHARE):
            order[total + j] = s * SHARE + j
        total = total + count[s]
    for j in range(BLK):
        order[total + j] = N_SLAB * SHARE
    env[pl.ds(N_SLAB * SHARE * 8, 8), :] = jnp.zeros((8, LANES), F32)

    def own_row(s, half):
        return (row8 + half * 8) * 8 + lax.rem(me - s + N_SLAB, N_SLAB)

    def geometry(s, half):
        before = lax.rem(s + N_SLAB - 1, N_SLAB)
        after = lax.rem(s + 1, N_SLAB)
        idx = nb[s, half * 8 : half * 8 + 8, :]
        low = idx & 127
        far = idx >= 128
        own = tile[s]
        edge = pltpu.roll(jnp.where(lane8 >= 64, tile[before], tile[after]), 64, 1)
        centre_at = own_row(s, half)
        base = s * SHARE + half * 8
        got = []
        for c in range(4):
            near = lanes_of(spread_rows(own[c : c + 1], 8), low)
            there = lanes_of(spread_rows(edge[4 + c : 5 + c], 8), low)
            got.append(jnp.where(far, there, near))
        mid = [lanes_of(spread_rows(own[c : c + 1], 8), centre_at) for c in range(4)]
        off = [got[c] - mid[c] for c in range(3)]
        d2 = off[0] * off[0] + off[1] * off[1] + off[2] * off[2]
        inv = lax.rsqrt(d2 + 0.25)
        fsw = jnp.where(idx >= 0, jnp.maximum(1.0 - d2 * (1.0 / 16.0), 0.0), 0.0)
        strength = fsw * fsw * inv
        si = strength * inv
        at = pl.ds(base, 8)
        for n, value in enumerate((*off, inv, fsw)):
            geo[n, at, :] = value
        for n, value in enumerate((strength, si * off[0], si * off[1], si * off[2], got[3], mid[3])):
            env[pl.ds(base * 8 + n, 8, stride=8), :] = value

    for s in range(N_SLAB):
        geometry(s, 0)

    def second_half(fn):
        def step(s, carry):
            @pl.when(count[s] > 8)
            def _():
                fn(s, 1)
            return carry

        lax.fori_loop(0, N_SLAB, step, 0)

    second_half(geometry)

    for load in loads[2:6]:
        load.wait()
    sc0, sc1, sh0, sh1 = 0, 1, 2, 3

    def forward(block, carry):
        first = block * BLK
        e, one, done = [], [], []
        for b in range(BLK):
            row = order[first + b]
            v = env[pl.ds(pl.multiple_of(row * 8, 8), 8), :]
            e.append(v)
            hyd = v[4:5] > 0.5
            sc = jnp.where(hyd, cols[sc1], cols[sc0])
            t = jnp.tanh(v[0:1] * sc + jnp.where(hyd, cols[sh1], cols[sh0]))
            one.append((t, (1.0 - t * t) * sc))
            hc[pl.ds(first + b, 1), :] = v[5:6]
        x = jnp.concatenate([a.astype(BF16) for pair in one for a in pair], axis=1)
        z = dot(w2t[...], x, NN)
        two = []
        for b in range(BLK):
            t1, d1 = one[b]
            t = jnp.tanh(z[:, 256 * b : 256 * b + 128])
            d = (1.0 - t * t) * z[:, 256 * b + 128 : 256 * b + 256]
            two.append((
                t + jnp.concatenate([t1[:24], t1[:24], t1[24:]], axis=0),
                d + jnp.concatenate([d1[:24], d1[:24], d1[24:]], axis=0),
            ))
        x = jnp.concatenate([a.astype(BF16) for pair in two for a in pair], axis=1)
        z = dot(w3t[...], x, NN)
        for b in range(BLK):
            t2, d2 = two[b]
            t = jnp.tanh(z[:, 256 * b : 256 * b + 128])
            d = (1.0 - t * t) * z[:, 256 * b + 128 : 256 * b + 256]
            l3 = (t + jnp.concatenate([t2[:48], t2[:48], t2[48:]], axis=0)).astype(BF16)
            d3 = (d + jnp.concatenate([d2[:48], d2[:48], d2[48:]], axis=0)).astype(BF16)
            three[first + b] = jnp.concatenate([l3, d3], axis=1)
            f = dot(e[b].astype(BF16), l3, NT) * (1.0 / 128.0)
            feats[pl.ds(pl.multiple_of((first + b) * 8, 8), 8), :] = jnp.concatenate(
                [f, jnp.zeros((8, 24), F32)], axis=1
            )
        return carry

    blocks = lax.div(total + (BLK - 1), BLK)
    lax.fori_loop(0, blocks, forward, 0)

    for load in loads[6:]:
        load.wait()

    lane_m = lax.broadcasted_iota(jnp.int32, (CHUNK, LANES), 1)

    def fit(chunk, carry):
        base = chunk * (CHUNK * 8)
        fs = [feats[pl.ds(base + c, CHUNK, stride=8), :] for c in range(4)]
        tiled = [lanes_of(f, lane_m & 15) for f in fs]
        spreads = [
            [lanes_of(f, spread_rows(spread[g : g + 1, :], CHUNK)) for f in fs] for g in range(13)
        ]
        desc = [sum(spreads[g][c] * tiled[c] for c in range(4)) for g in range(13)]
        desc = jnp.concatenate(desc, axis=1).astype(BF16)[:, :1600]
        f1 = jnp.tanh(dot(desc, fit1[...], NT) + c1[...])
        t2 = jnp.tanh(dot(f1.astype(BF16), fit2[...], NN) + c2[...])
        f2 = t2 + f1
        t3 = jnp.tanh(dot(f2.astype(BF16), fit3[...], NN) + c3[...])
        h = hc[pl.ds(chunk * CHUNK, CHUNK), :]
        h = jnp.concatenate([h, h], axis=1)[:, :240]
        g3 = readout[0:1, :] + h * (readout[1:2, :] - readout[0:1, :])
        g2 = g3 + dot((g3 * (1.0 - t3 * t3)).astype(BF16), fit3[...], NT)
        g1 = g2 + dot((g2 * (1.0 - t2 * t2)).astype(BF16), fit2[...], NT)
        gd = dot((g1 * (1.0 - f1 * f1)).astype(BF16), fit1[...], NN)
        gd = jnp.concatenate([gd, jnp.zeros((CHUNK, 64), F32)], axis=1)
        parts = [gd[:, g * LANES : (g + 1) * LANES] for g in range(13)]
        for c in range(4):
            left = jnp.concatenate([p * tiled[c] for p in parts], axis=1).astype(BF16)
            left = dot(left, fold[...], NN)
            right = sum(parts[g] * spreads[g][c] for g in range(13))
            for shift in (64, 32, 16):
                right = right + pltpu.roll(right, shift, 1)
            gf = left + jnp.where(lane_m < 16, right, 0.0)
            gfeats[pl.ds(base + c, CHUNK, stride=8), :] = gf * (1.0 / 128.0)
        return carry

    lax.fori_loop(0, lax.div(total + (CHUNK - 1), CHUNK), fit, 0)

    def back(block, carry):
        first = block * BLK
        for b in range(BLK):
            row = order[first + b]
            gf = gfeats[pl.ds(pl.multiple_of((first + b) * 8, 8), 8), :][:, :104]
            qp = dot(gf.astype(BF16), three[first + b], NN)
            at = pl.ds(pl.multiple_of(row * 8, 8), 8)
            qs[at, :] = qp[:, :128]
            ps[at, :] = qp[:, 128:]
        return carry

    lax.fori_loop(0, blocks, back, 0)

    sub = lax.broadcasted_iota(jnp.int32, (LANES, LANES), 0)

    def scatter(s, half):
        base = s * SHARE + half * 8
        at = pl.ds(base, 8)
        idx = nb[s, half * 8 : half * 8 + 8, :]
        off = [geo[n, at, :] for n in range(3)]
        inv, fsw = geo[3, at, :], geo[4, at, :]
        q = [qs[pl.ds(base * 8 + n, 8, stride=8), :] for n in range(4)]
        p = [ps[pl.ds(base * 8 + n, 8, stride=8), :] for n in range(4)]
        inv3 = 0.5 * inv * inv * inv
        strength = fsw * fsw * inv
        qo = q[1] * off[0] + q[2] * off[1] + q[3] * off[2]
        po = p[1] * off[0] + p[2] * off[1] + p[3] * off[2]
        gs = q[0] + inv * qo + strength * (p[0] + inv * po)
        gd2 = -gs * (fsw * inv * 0.125 + fsw * fsw * inv3) - qo * strength * inv3
        si = strength * inv
        g = [jnp.where(idx >= 0, q[1 + c] * si + 2.0 * off[c] * gd2, 0.0) for c in range(3)]
        near = idx < 128
        centre_at = own_row(s, half) == lane8
        grad = jnp.zeros((8, LANES), F32)
        for c in range(3):
            scat[pl.ds(base * 8 + c, 8, stride=8), :] = jnp.where(near, g[c], 0.0)
            scat[pl.ds(base * 8 + 3 + c, 8, stride=8), :] = jnp.where(near, 0.0, g[c])
            total_c = jnp.sum(g[c], axis=1, keepdims=True)
            line = jnp.sum(jnp.where(centre_at, -total_c, 0.0), axis=0, keepdims=True)
            grad = jnp.where(row8 == c, line, grad)
        lhs, rhs = [], []
        for j in range(8):
            lhs.append(scat[pl.ds((base + j) * 8, 8), :].astype(BF16))
            low = nb[s, half * 8 + j : half * 8 + j + 1, :] & 127
            rhs.append(jnp.where(sub == low, 1.0, 0.0).astype(BF16))
        grad = grad + dot(jnp.concatenate(lhs, axis=1), jnp.concatenate(rhs, axis=1), NT)
        if half == 0:
            feats[pl.ds(s * 8, 8), :] = grad
        else:
            feats[pl.ds(s * 8, 8), :] += grad

    for s in range(N_SLAB):
        scatter(s, 0)
    second_half(scatter)
    grads = [feats[pl.ds(s * 8, 8), :] for s in range(N_SLAB)]
    for s in range(N_SLAB):
        edge = jnp.where(lane8 < 64, grads[(s + 1) % N_SLAB], grads[(s - 1) % N_SLAB])
        out[s] = jnp.where(row8 < 3, grads[s], edge)


def force_call(tile, nb, w2t, w3t, cols, fit):
    fit1, b1, fit2, b2, fit3, b3, readout = fit
    _, _, _, _, _, spread, fold = selections()
    rows = N_SLAB * SHARE
    operands = (
        tile, nb, w2t, w3t, cols, jnp.asarray(spread), b1[None], b2[None], b3[None], readout,
        fit1.T, fit2, fit3, jnp.asarray(fold, BF16),
    )
    return pl.pallas_call(
        force_kernel,
        out_shape=jax.ShapeDtypeStruct((N_SLAB, 8, LANES), F32),
        in_specs=[pl.BlockSpec(memory_space=PLACE)] * len(operands),
        out_specs=pl.BlockSpec(memory_space=pltpu.VMEM),
        scratch_shapes=[pltpu.VMEM(x.shape, x.dtype) for x in operands] + [
            pltpu.VMEM(((rows + 1) * 8, LANES), F32),
            pltpu.VMEM((5, rows, LANES), F32),
            pltpu.SMEM((rows + 24,), jnp.int32),
            pltpu.SMEM((N_SLAB,), jnp.int32),
            pltpu.VMEM((rows + 8, LANES), F32),
            pltpu.VMEM((rows + 8, 104, 256), BF16),
            pltpu.VMEM(((rows + 8) * 8, LANES), F32),
            pltpu.VMEM(((rows + 8) * 8, LANES), F32),
            pltpu.VMEM(((rows + 1) * 8, LANES), F32),
            pltpu.VMEM(((rows + 1) * 8, LANES), F32),
            pltpu.VMEM((rows * 8, LANES), F32),
            pltpu.SemaphoreType.DMA((len(operands),)),
        ],
        name="force",
    )(*operands)


MESH = pl.DeviceIdType.MESH
NZ = 16
NY = 4
REACH = 4


def hail(peers):
    barrier = pltpu.get_barrier_semaphore()
    for peer in peers:
        pl.semaphore_signal(barrier, inc=1, device_id=peer, device_id_type=MESH)


def meet(peers):
    pl.semaphore_wait(pltpu.get_barrier_semaphore(), len(peers))


def send(src, dst, out_sem, in_sem, peer):
    copy = pltpu.make_async_remote_copy(
        src_ref=src, dst_ref=dst, send_sem=out_sem, recv_sem=in_sem, device_id=peer, device_id_type=MESH
    )
    copy.start()
    return copy


def slab_peers():
    me = lax.axis_index("slab")
    return me, [{"slab": lax.rem(me + i, N_SLAB)} for i in range(1, N_SLAB)]


def exchange_kernel(*refs):
    pos_in, types_in, halo_in, lists = refs[:4]
    weights, (tiles, nb), results = refs[4:15], refs[15:17], refs[17:20]
    pos, types, halo = refs[20:23]
    held, made, mine = refs[23:34], refs[34:37], refs[37]
    tile_out, tile_in, list_out, list_in, own_sems, load_sems = refs[38:]
    me, peers = slab_peers()
    hail(peers)
    first = fetch([(pos_in, pos), (types_in, types), (halo_in, halo)], load_sems)
    later = fetch(list(zip(weights, held)), load_sems, 3)
    for load in first:
        load.wait()
    mine[...] = own_tile(pos[:, 0, :], types[...], halo[...])
    meet(peers)
    copies = []
    for i, peer in enumerate(peers):
        copies.append(send(lists.at[:, i + 1, :], nb.at[me], list_out.at[i], list_in.at[i], peer))
    for i, peer in enumerate(peers):
        copies.append(send(mine, tiles.at[me], tile_out.at[i], tile_in.at[i], peer))
    own = fetch([(lists.at[:, 0, :], nb.at[me]), (mine, tiles.at[me])], own_sems)
    for load in later:
        load.wait()
    prepare_weights(*held, *made)
    own += fetch(list(zip(made, results)), own_sems, 2)
    for copy in own + copies:
        copy.wait()


def finish_kernel(
    msgs, pos_in, vel_in, types_in, halo_in, coefs_in, out,
    mine, pos, vel, types, halo, coefs, inbox, ring, mixed, ybox, result,
    slab_out, slab_in, ring_out, ring_in, far_out, far_in, y_out, y_in, load_sems,
):
    me, peers = slab_peers()
    bead = lax.axis_index("bead")
    z, y = lax.div(bead, NY), lax.rem(bead, NY)

    def along(d):
        return {"bead": lax.rem(z + NZ + d, NZ) * NY + y}

    steps = [d for k in range(1, REACH + 1) for d in (k, -k)]
    yet = [lax.rem(y + k, NY) for k in range(1, NY)]
    ypeers = [{"bead": z * NY + other} for other in yet]
    everyone = [along(d) for d in steps[::-1]] + peers + ypeers
    hail(everyone)
    loads = fetch(
        [
            (msgs.at[me], mine), (pos_in, pos), (vel_in, vel), (types_in, types), (halo_in, halo),
            (coefs_in.at[y], coefs),
        ],
        load_sems,
    )
    for load in loads:
        load.wait()
    bins = pltpu.roll(spread_rows(halo[...], 8), 64, 1)[0:1]
    hit = jnp.where(lax.broadcasted_iota(jnp.int32, (LANES, LANES), 0) == bins, 1.0, 0.0)
    meet(everyone)

    copies = [
        send(msgs.at[lax.rem(me + i + 1, N_SLAB)], inbox.at[i], slab_out.at[i], slab_in.at[i], peer)
        for i, peer in enumerate(peers)
    ]
    got = mine[...]
    for i, copy in enumerate(copies):
        copy.wait()
        got = got + inbox[i]
    back = lax.dot_general(got, hit, NT, preferred_element_type=F32, precision=HIGH)
    force = -(got[0:3] + back[3:6])
    kicked = vel[:, 0, :] + STEP * jnp.where(types[...] == 1, 1.0, 1.0 / HEAVY) * force
    own = ring.at[8]
    own[...] = jnp.concatenate([pos[:, 0, :], kicked, jnp.zeros((2, LANES), F32)], axis=0)

    near = {
        d: send(own, ring.at[8 - d], ring_out.at[n], ring_in.at[n], along(d)) for n, d in enumerate(steps)
    }
    result[6:9, 0, :] = force
    for d in steps:
        if d > 0:
            near[d].wait_recv()
    up = send(ring.at[pl.ds(4, 4)], ring.at[pl.ds(0, 4)], far_out.at[0], far_in.at[0], along(REACH))
    for d in steps:
        if d < 0:
            near[d].wait_recv()
    down = send(ring.at[pl.ds(9, 3)], ring.at[pl.ds(13, 3)], far_out.at[1], far_in.at[1], along(-REACH))
    NN = (((1,), (0,)), ((), ()))
    dot = functools.partial(lax.dot_general, preferred_element_type=F32, precision=HIGH)
    table = coefs[...]
    sums = dot(table[:, 32:104], jnp.concatenate([ring[n] for n in range(4, 13)], axis=0), NN)
    for d in steps:
        near[d].wait_send()
    up.wait()
    down.wait()
    rest = [ring[n] for n in (0, 1, 2, 3, 13, 14, 15)]
    sums = sums + dot(
        jnp.concatenate([table[:, :32], table[:, 104:]], axis=1), jnp.concatenate(rest, axis=0), NN
    )
    for k in range(NY):
        mixed[k] = sums[8 * k : 8 * k + 8]
    copies = [
        send(mixed.at[other], ybox.at[i], y_out.at[i], y_in.at[i], peer)
        for i, (other, peer) in enumerate(zip(yet, ypeers))
    ]
    done = mixed[y]
    for i, copy in enumerate(copies):
        copy.wait()
        done = done + ybox[i]
    result[0:6, 0, :] = done[0:6]
    last = pltpu.make_async_copy(result, out, load_sems.at[0])
    last.start()
    last.wait()


def ring_coefficients():
    cos, travel, spring = (m[:, 0].astype(np.float64) for m in mode_matrices())
    table = np.zeros((NY, NY, 8, NZ, 8), np.float32)
    for y in range(NY):
        for to in range(NY):
            for slot in range(NZ):
                apart = (to - y - NY * (slot - 8)) % BEADS
                for c in range(3):
                    table[y, to, c, slot, c] = cos[apart]
                    table[y, to, c, slot, 3 + c] = travel[apart]
                    table[y, to, 3 + c, slot, c] = -spring[apart]
                    table[y, to, 3 + c, slot, 3 + c] = cos[apart]
    return table.reshape(NY, NY * 8, NZ * 8)


def dmas(n):
    return pltpu.SemaphoreType.DMA((n,))


def like(x):
    return pltpu.VMEM(x.shape, x.dtype)


def finish_call(msgs, pos, vel, types, halo):
    near = 2 * REACH
    place = pl.BlockSpec(memory_space=PLACE)
    return pl.pallas_call(
        finish_kernel,
        out_shape=jax.ShapeDtypeStruct((9, 1, LANES), F32),
        in_specs=[place] * 6,
        out_specs=place,
        scratch_shapes=[
            pltpu.VMEM((8, LANES), F32),
            like(pos), like(vel), like(types), like(halo),
            pltpu.VMEM((NY * 8, NZ * 8), F32),
            pltpu.VMEM((7, 8, LANES), F32),
            pltpu.VMEM((NZ, 8, LANES), F32),
            pltpu.VMEM((NY, 8, LANES), F32),
            pltpu.VMEM((NY - 1, 8, LANES), F32),
            pltpu.VMEM((9, 1, LANES), F32),
            dmas(7), dmas(7), dmas(near), dmas(near), dmas(2), dmas(2), dmas(NY - 1), dmas(NY - 1), dmas(6),
        ],
        compiler_params=pltpu.CompilerParams(collective_id=1, has_side_effects=True),
        name="finish",
    )(msgs, pos, vel, types, halo, jnp.asarray(ring_coefficients()))


def local(
    positions, velocities, atom_types, live_atoms, halo_rows, neighbours,
    type_scale, type_shift, embed_two, embed_bias_two, embed_three, embed_bias_three,
    fit_first, fit_bias_first, fit_second, fit_bias_second, fit_third, fit_bias_third, fit_readout,
):
    del live_atoms
    types = atom_types[None]
    s1, a2, p1, a3, p2, _, _ = selections()
    place = pl.BlockSpec(memory_space=PLACE)
    weights = (
        type_scale, type_shift, embed_two, embed_bias_two[None], embed_three, embed_bias_three[None],
        jnp.asarray(s1), jnp.asarray(a2, BF16), jnp.asarray(p1, BF16), jnp.asarray(a3, BF16),
        jnp.asarray(p2, BF16),
    )
    made = (
        jax.ShapeDtypeStruct((56, 32), BF16),
        jax.ShapeDtypeStruct((104, 56), BF16),
        jax.ShapeDtypeStruct((4, 32, LANES), F32),
    )
    firsts = (positions, types, halo_rows)
    tiles, nb, w2t, w3t, cols = pl.pallas_call(
        exchange_kernel,
        out_shape=(
            jax.ShapeDtypeStruct((N_SLAB, 8, LANES), F32),
            jax.ShapeDtypeStruct((N_SLAB, SHARE, LANES), jnp.int32),
        ) + made,
        in_specs=[place] * 15,
        out_specs=(place,) * 5,
        scratch_shapes=[like(x) for x in firsts + weights + made] + [
            pltpu.VMEM((8, LANES), F32), dmas(7), dmas(7), dmas(7), dmas(7), dmas(5), dmas(14),
        ],
        compiler_params=pltpu.CompilerParams(collective_id=0, has_side_effects=True),
        name="exchange",
    )(*firsts, neighbours.reshape(SHARE, N_SLAB, LANES), *weights)
    msgs = force_call(
        tiles, nb, w2t, w3t, cols,
        (fit_first, fit_bias_first, fit_second, fit_bias_second, fit_third, fit_bias_third, fit_readout),
    )
    out = finish_call(msgs, positions, velocities, types, halo_rows)
    return out[0:3], out[3:6], out[6:9]


def solution(mesh):
    wide = P(None, "bead", "slab")
    return jax.shard_map(
        local,
        mesh=mesh,
        in_specs=(wide, wide, P("slab"), P("slab"), P("slab", None), P("slab", None)) + (P(),) * 13,
        out_specs=(wide, wide, wide),
        check_vma=False,
    )
```

```python
import functools

import jax
import jax.numpy as jnp
import numpy as np
from jax import lax
from jax.experimental import pallas as pl
from jax.experimental.pallas import tpu as pltpu
from jax.sharding import PartitionSpec as P

BEADS = 64
N_SLAB = 8
SHARE = 16
LANES = 128
STEP = 0.25
HEAVY = 16.0
BLK = 16
BACK = 32
MXU_GROUPS = 8
CHUNK = 64
F32 = jnp.float32
BF16 = jnp.bfloat16
NT = (((1,), (1,)), ((), ()))
HIGH = lax.Precision.HIGHEST
PLACE = pltpu.HBM


def two_feature(row):
    if row < 24:
        return row
    if row < 48:
        return row + 1
    if row < 52:
        return (24, 49)[(row - 48) % 2]
    return -1


def three_feature(row):
    if row < 48:
        return two_feature(row)
    if row < 96:
        return 50 + two_feature(row - 48)
    if row < 100:
        return (24, 49, 74, 99)[row - 96]
    return -1


def selections():
    one_of = [k if k < 24 else 24 if k < 28 else -1 for k in range(32)]
    s1 = np.zeros((32, 25), np.float32)
    for k, f in enumerate(one_of):
        if f >= 0:
            s1[k, f] = 1
    a2 = np.zeros((56, 50), np.float32)
    for k in range(56):
        if two_feature(k) >= 0:
            a2[k, two_feature(k)] = 1
    b1 = np.zeros((25, 32), np.float32)
    for f in range(25):
        b1[f, f] = 1
    a3 = np.zeros((104, 100), np.float32)
    where = np.zeros((104,), np.int32)
    where[100:] = 127
    for k in range(104):
        if three_feature(k) >= 0:
            a3[k, three_feature(k)] = 1
            where[three_feature(k)] = k
    b2 = np.zeros((50, 56), np.float32)
    for k in range(50):
        b2[two_feature(k), k] = 1
    fold = np.zeros((14 * LANES, LANES), np.float32)
    places = np.full((16, LANES), 127, np.int32)
    for lane in range(1600):
        fold[lane, where[lane // 16]] = 1
        places[lane // LANES, lane % LANES] = where[lane // 16]
    for lane in range(LANES):
        fold[13 * LANES + lane, lane % 16] = 1
    return s1, a2, b1, a3, b2, places, fold


def mode_matrices():
    n = BEADS
    j, k = np.arange(n)[:, None], np.arange(n)[None, :]
    angle = 2 * np.pi * ((j * k) % n) / n
    basis = np.where(
        k == 0,
        1 / np.sqrt(n),
        np.where(
            k < n // 2,
            np.sqrt(2 / n) * np.cos(angle),
            np.where(k == n // 2, np.where(j % 2 == 0, 1.0, -1.0) / np.sqrt(n), np.sqrt(2 / n) * np.sin(angle)),
        ),
    )
    sine = np.sin(np.pi * np.arange(n) / n)
    ratio = 2 * sine
    theta = 1.2 * n * sine
    travel = np.where(np.arange(n) == 0, 1.0, np.sin(theta) / np.where(np.arange(n) == 0, 1.0, ratio))
    return tuple(
        ((basis * d[None, :]) @ basis.T).astype(np.float32)
        for d in (np.cos(theta), travel, ratio * np.sin(theta))
    )


def lanes_of(table, index):
    return jnp.take_along_axis(table, index, axis=1, mode="promise_in_bounds")


def spread_rows(row, count):
    return jnp.broadcast_to(row, (count, row.shape[1]))


def own_tile(pos, types, halo):
    hydrogen = jnp.where(types == 1, 1.0, 0.0).astype(F32)
    mine = jnp.concatenate([pos, hydrogen], axis=0)
    wide = jnp.concatenate([mine, mine], axis=0)
    sent = lanes_of(wide, spread_rows(halo, 8))
    return jnp.where(lax.broadcasted_iota(jnp.int32, (8, LANES), 0) < 4, wide, sent)


def thirds(row):
    high = row.astype(BF16).astype(F32)
    rest = row - high
    mid = rest.astype(BF16).astype(F32)
    return high, mid, rest - mid


def bias_rows(bias, first, count):
    high, mid, low = thirds(bias)
    at = lax.broadcasted_iota(jnp.int32, (count, bias.shape[1]), 0)
    return jnp.where(at == first, high, jnp.where(at == first + 1, mid, jnp.where(at == first + 2, low, 0.0)))


def prepare_weights(scale, shift, w2, b2, w3, b3, s1, a2, p1, a3, p2, w2t, w3t, cols):
    dot = functools.partial(lax.dot_general, preferred_element_type=F32)
    two = dot(a2[...], w2[...], NT).astype(BF16)
    two = dot(two, p1[...], (((1,), (0,)), ((), ())))
    two = two + dot(a2[...], bias_rows(b2[...], 28, 32).astype(BF16), NT)
    w2t[...] = two.astype(BF16)
    three = dot(a3[...], w3[...], NT).astype(BF16)
    three = dot(three, p2[...], (((1,), (0,)), ((), ())))
    three = three + dot(a3[...], bias_rows(b3[...], 52, 56).astype(BF16), NT)
    w3t[...] = three.astype(BF16)
    at = lax.broadcasted_iota(jnp.int32, (32, LANES), 0)
    ones = jnp.where((at >= 28) & (at < 31), 20.0, 0.0)
    for kind in range(2):
        for n, ref in enumerate((scale, shift)):
            col = dot(s1[...], spread_rows(ref[kind : kind + 1, :], LANES), NT, precision=HIGH)
            cols[2 * n + kind] = col + ones if n else col


def fetch(pairs, sems, first=0):
    loads = [pltpu.make_async_copy(src, dst, sems.at[first + n]) for n, (src, dst) in enumerate(pairs)]
    for load in loads:
        load.start()
    return loads


def force_kernel(*refs):
    given, out, held, rest = refs[:14], refs[14], refs[15:29], refs[29:]
    (
        tile, nb, w2t, w3t, cols, places, c1, c2, c3, readout, fit1, fit2, fit3, fold,
    ) = held
    env, geo, order, count, hc, three, feats, gfeats, qs, ps, scat, sems = rest
    me = lax.axis_index("slab")
    loads = fetch(list(zip(given, held)), sems)
    for load in loads[:2]:
        load.wait()
    dot = functools.partial(lax.dot_general, preferred_element_type=F32)
    NN = (((1,), (0,)), ((), ()))
    lane8 = lax.broadcasted_iota(jnp.int32, (8, LANES), 1)
    row8 = lax.broadcasted_iota(jnp.int32, (8, LANES), 0)

    for s in range(N_SLAB):
        count[s] = jnp.sum(jnp.where(nb[s][:, 0:1] >= 0, 1.0, 0.0)).astype(jnp.int32)
    total = jnp.int32(0)
    for s in range(N_SLAB):
        for j in range(SHARE):
            order[total + j] = s * SHARE + j
        total = total + count[s]
    for j in range(max(BLK, BACK)):
        order[total + j] = N_SLAB * SHARE
    env[pl.ds(N_SLAB * SHARE * 8, 8), :] = jnp.zeros((8, LANES), F32)

    def own_row(s, half):
        return (row8 + half * 8) * 8 + lax.rem(me - s + N_SLAB, N_SLAB)

    def geometry(s, half):
        before = lax.rem(s + N_SLAB - 1, N_SLAB)
        after = lax.rem(s + 1, N_SLAB)
        idx = nb[s, half * 8 : half * 8 + 8, :]
        low = idx & 127
        far = idx >= 128
        own = tile[s]
        edge = pltpu.roll(jnp.where(lane8 >= 64, tile[before], tile[after]), 64, 1)
        centre_at = own_row(s, half)
        base = s * SHARE + half * 8
        got = []
        for c in range(4):
            near = lanes_of(spread_rows(own[c : c + 1], 8), low)
            there = lanes_of(spread_rows(edge[4 + c : 5 + c], 8), low)
            got.append(jnp.where(far, there, near))
        mid = [lanes_of(spread_rows(own[c : c + 1], 8), centre_at) for c in range(4)]
        off = [got[c] - mid[c] for c in range(3)]
        d2 = off[0] * off[0] + off[1] * off[1] + off[2] * off[2]
        inv = lax.rsqrt(d2 + 0.25)
        fsw = jnp.where(idx >= 0, jnp.maximum(1.0 - d2 * (1.0 / 16.0), 0.0), 0.0)
        strength = fsw * fsw * inv
        si = strength * inv
        at = pl.ds(base, 8)
        for n, value in enumerate((*off, inv, fsw)):
            geo[n, at, :] = value
        for n, value in enumerate((strength, si * off[0], si * off[1], si * off[2], got[3], mid[3])):
            env[pl.ds(base * 8 + n, 8, stride=8), :] = value

    for s in range(N_SLAB):
        geometry(s, 0)

    def second_half(fn):
        def step(s, carry):
            @pl.when(count[s] > 8)
            def _():
                fn(s, 1)
            return carry

        lax.fori_loop(0, N_SLAB, step, 0)

    second_half(geometry)

    for load in loads[2:6]:
        load.wait()
    sc0, sc1, sh0, sh1 = 0, 1, 2, 3

    def forward(block, carry):
        first = block * BLK
        e, one, done = [], [], []
        for b in range(BLK):
            row = order[first + b]
            v = env[pl.ds(pl.multiple_of(row * 8, 8), 8), :]
            e.append(v)
            hyd = v[4:5] > 0.5
            sc = jnp.where(hyd, cols[sc1], cols[sc0])
            t = jnp.tanh(v[0:1] * sc + jnp.where(hyd, cols[sh1], cols[sh0]))
            one.append((t, (1.0 - t * t) * sc))
            hc[pl.ds(first + b, 1), :] = v[5:6]
        x = jnp.concatenate([a.astype(BF16) for pair in one for a in pair], axis=1)
        z = dot(w2t[...], x, NN)
        two = []
        for b in range(BLK):
            t1, d1 = one[b]
            t = jnp.tanh(z[:, 256 * b : 256 * b + 128])
            d = (1.0 - t * t) * z[:, 256 * b + 128 : 256 * b + 256]
            two.append((
                (t + jnp.concatenate([t1[:24], t1[:24], t1[24:]], axis=0)).astype(BF16),
                (d + jnp.concatenate([d1[:24], d1[:24], d1[24:]], axis=0)).astype(BF16),
            ))
        x = jnp.concatenate([a for pair in two for a in pair], axis=1)
        z = dot(w3t[...], x, NN)
        for b in range(BLK):
            t2, d2 = two[b]
            t = jnp.tanh(z[:, 256 * b : 256 * b + 128].astype(BF16))
            d = (1 - t * t) * z[:, 256 * b + 128 : 256 * b + 256].astype(BF16)
            l3 = t + jnp.concatenate([t2[:48], t2[:48], t2[48:]], axis=0)
            d3 = d + jnp.concatenate([d2[:48], d2[:48], d2[48:]], axis=0)
            three[first + b] = jnp.concatenate([l3, d3], axis=1)
            f = dot(e[b].astype(BF16), l3, NT) * (1.0 / 128.0)
            feats[pl.ds(pl.multiple_of((first + b) * 8, 8), 8), :] = jnp.concatenate(
                [f, jnp.zeros((8, 24), F32)], axis=1
            )
        return carry

    blocks = lax.div(total + (BLK - 1), BLK)
    lax.fori_loop(0, blocks, forward, 0)

    for load in loads[6:]:
        load.wait()

    lane_m = lax.broadcasted_iota(jnp.int32, (CHUNK, LANES), 1)

    def fit(chunk, carry):
        base = chunk * (CHUNK * 8)
        fs = [feats[pl.ds(base + c, CHUNK, stride=8), :] for c in range(4)]
        stack = jnp.concatenate(fs, axis=0).astype(BF16)
        picks = dot(stack, fold[: MXU_GROUPS * LANES], NT)
        tiled = [lanes_of(f, lane_m & 15) for f in fs]
        spreads = [
            [picks[CHUNK * c : CHUNK * (c + 1), g * LANES : (g + 1) * LANES] for g in range(MXU_GROUPS)]
            + [lanes_of(fs[c], spread_rows(places[g : g + 1, :], CHUNK)) for g in range(MXU_GROUPS, 13)]
            for c in range(4)
        ]
        desc = [sum(spreads[c][g] * tiled[c] for c in range(4)).astype(BF16) for g in range(13)]
        desc = jnp.concatenate(desc, axis=1)[:, :1600]
        short = [v.astype(BF16) for v in tiled]
        f1 = jnp.tanh(dot(desc, fit1[...], NT) + c1[...])
        t2 = jnp.tanh(dot(f1.astype(BF16), fit2[...], NN) + c2[...])
        f2 = t2 + f1
        t3 = jnp.tanh(dot(f2.astype(BF16), fit3[...], NN) + c3[...])
        h = hc[pl.ds(chunk * CHUNK, CHUNK), :]
        h = jnp.concatenate([h, h], axis=1)[:, :240]
        g3 = readout[0:1, :] + h * (readout[1:2, :] - readout[0:1, :])
        g2 = g3 + dot((g3 * (1.0 - t3 * t3)).astype(BF16), fit3[...], NT)
        g1 = g2 + dot((g2 * (1.0 - t2 * t2)).astype(BF16), fit2[...], NT)
        gd = dot((g1 * (1.0 - f1 * f1)).astype(BF16), fit1[...], NN)
        gd = jnp.concatenate([gd, jnp.zeros((CHUNK, 64), F32)], axis=1)
        parts = [gd[:, g * LANES : (g + 1) * LANES] for g in range(13)]
        left = [jnp.concatenate([p.astype(BF16) * v for p in parts], axis=1) for v in short]
        gf = dot(jnp.concatenate(left, axis=0), fold[: 13 * LANES], NN)
        right = [sum(parts[g] * spreads[c][g] for g in range(13)) for c in range(4)]
        gf = gf + dot(jnp.concatenate(right, axis=0).astype(BF16), fold[13 * LANES :], NN)
        for c in range(4):
            part = gf[CHUNK * c : CHUNK * (c + 1)] * (1.0 / 128.0)
            gfeats[pl.ds(base + c, CHUNK, stride=8), :] = part
        return carry

    lax.fori_loop(0, lax.div(total + (CHUNK - 1), CHUNK), fit, 0)

    def back(block, carry):
        first = block * BACK
        for b in range(BACK):
            row = order[first + b]
            gf = gfeats[pl.ds(pl.multiple_of((first + b) * 8, 8), 8), :][:, :104]
            qp = dot(gf.astype(BF16), three[first + b], NN)
            at = pl.ds(pl.multiple_of(row * 8, 8), 8)
            qs[at, :] = qp[:, :128]
            ps[at, :] = qp[:, 128:]
        return carry

    lax.fori_loop(0, lax.div(total + (BACK - 1), BACK), back, 0)

    sub = lax.broadcasted_iota(jnp.int32, (LANES, LANES), 0).astype(F32).astype(BF16)

    def scatter(s, half):
        base = s * SHARE + half * 8
        at = pl.ds(base, 8)
        idx = nb[s, half * 8 : half * 8 + 8, :]
        off = [geo[n, at, :] for n in range(3)]
        inv, fsw = geo[3, at, :], geo[4, at, :]
        q = [qs[pl.ds(base * 8 + n, 8, stride=8), :] for n in range(4)]
        p = [ps[pl.ds(base * 8 + n, 8, stride=8), :] for n in range(4)]
        inv3 = 0.5 * inv * inv * inv
        strength = fsw * fsw * inv
        qo = q[1] * off[0] + q[2] * off[1] + q[3] * off[2]
        po = p[1] * off[0] + p[2] * off[1] + p[3] * off[2]
        gs = q[0] + inv * qo + strength * (p[0] + inv * po)
        gd2 = -gs * (fsw * inv * 0.125 + fsw * fsw * inv3) - qo * strength * inv3
        si = strength * inv
        g = [jnp.where(idx >= 0, q[1 + c] * si + 2.0 * off[c] * gd2, 0.0) for c in range(3)]
        near = idx < 128
        centre_at = own_row(s, half) == lane8
        grad = jnp.zeros((8, LANES), F32)
        for c in range(3):
            scat[pl.ds(base * 8 + c, 8, stride=8), :] = jnp.where(near, g[c], 0.0)
            scat[pl.ds(base * 8 + 3 + c, 8, stride=8), :] = jnp.where(near, 0.0, g[c])
            total_c = jnp.sum(g[c], axis=1, keepdims=True)
            line = jnp.sum(jnp.where(centre_at, -total_c, 0.0), axis=0, keepdims=True)
            grad = jnp.where(row8 == c, line, grad)
        lhs, rhs = [], []
        for j in range(8):
            lhs.append(scat[pl.ds((base + j) * 8, 8), :].astype(BF16))
            low = nb[s, half * 8 + j : half * 8 + j + 1, :] & 127
            low = spread_rows(low.astype(F32).astype(BF16), LANES)
            rhs.append(jnp.where(sub == low, jnp.ones_like(sub), jnp.zeros_like(sub)))
        grad = grad + dot(jnp.concatenate(lhs, axis=1), jnp.concatenate(rhs, axis=1), NT)
        if half == 0:
            feats[pl.ds(s * 8, 8), :] = grad
        else:
            feats[pl.ds(s * 8, 8), :] += grad

    for s in range(N_SLAB):
        scatter(s, 0)
    second_half(scatter)
    grads = [feats[pl.ds(s * 8, 8), :] for s in range(N_SLAB)]
    for s in range(N_SLAB):
        edge = jnp.where(lane8 < 64, grads[(s + 1) % N_SLAB], grads[(s - 1) % N_SLAB])
        out[s] = jnp.where(row8 < 3, grads[s], edge)


def force_call(tile, nb, w2t, w3t, cols, fit):
    fit1, b1, fit2, b2, fit3, b3, readout = fit
    places, fold = selections()[-2:]
    rows = N_SLAB * SHARE
    operands = (
        tile, nb, w2t, w3t, cols, jnp.asarray(places), b1[None], b2[None], b3[None], readout,
        fit1.T, fit2, fit3, jnp.asarray(fold, BF16),
    )
    return pl.pallas_call(
        force_kernel,
        out_shape=jax.ShapeDtypeStruct((N_SLAB, 8, LANES), F32),
        in_specs=[pl.BlockSpec(memory_space=PLACE)] * len(operands),
        out_specs=pl.BlockSpec(memory_space=pltpu.VMEM),
        scratch_shapes=[pltpu.VMEM(x.shape, x.dtype) for x in operands] + [
            pltpu.VMEM(((rows + 1) * 8, LANES), F32),
            pltpu.VMEM((5, rows, LANES), F32),
            pltpu.SMEM((rows + 48,), jnp.int32),
            pltpu.SMEM((N_SLAB,), jnp.int32),
            pltpu.VMEM((rows + 32, LANES), F32),
            pltpu.VMEM((rows + 32, 104, 256), BF16),
            pltpu.VMEM(((rows + 32) * 8, LANES), F32),
            pltpu.VMEM(((rows + 32) * 8, LANES), F32),
            pltpu.VMEM(((rows + 1) * 8, LANES), F32),
            pltpu.VMEM(((rows + 1) * 8, LANES), F32),
            pltpu.VMEM((rows * 8, LANES), F32),
            pltpu.SemaphoreType.DMA((len(operands),)),
        ],
        name="force",
    )(*operands)


MESH = pl.DeviceIdType.MESH
NZ = 16
NY = 4
REACH = 4


def hail(peers):
    barrier = pltpu.get_barrier_semaphore()
    for peer in peers:
        pl.semaphore_signal(barrier, inc=1, device_id=peer, device_id_type=MESH)


def meet(peers):
    pl.semaphore_wait(pltpu.get_barrier_semaphore(), len(peers))


def send(src, dst, out_sem, in_sem, peer):
    copy = pltpu.make_async_remote_copy(
        src_ref=src, dst_ref=dst, send_sem=out_sem, recv_sem=in_sem, device_id=peer, device_id_type=MESH
    )
    copy.start()
    return copy


def slab_peers():
    me = lax.axis_index("slab")
    return me, [{"slab": lax.rem(me + i, N_SLAB)} for i in range(1, N_SLAB)]


def exchange_kernel(*refs):
    pos_in, types_in, halo_in, lists = refs[:4]
    weights, (tiles, nb), results = refs[4:15], refs[15:17], refs[17:20]
    pos, types, halo = refs[20:23]
    held, made, mine = refs[23:34], refs[34:37], refs[37]
    tile_out, tile_in, list_out, list_in, own_sems, load_sems = refs[38:]
    me, peers = slab_peers()
    hail(peers)
    first = fetch([(pos_in, pos), (types_in, types), (halo_in, halo)], load_sems)
    later = fetch(list(zip(weights, held)), load_sems, 3)
    for load in first:
        load.wait()
    mine[...] = own_tile(pos[:, 0, :], types[...], halo[...])
    meet(peers)
    copies = []
    for i, peer in enumerate(peers):
        copies.append(send(lists.at[:, i + 1, :], nb.at[me], list_out.at[i], list_in.at[i], peer))
    for i, peer in enumerate(peers):
        copies.append(send(mine, tiles.at[me], tile_out.at[i], tile_in.at[i], peer))
    own = fetch([(lists.at[:, 0, :], nb.at[me]), (mine, tiles.at[me])], own_sems)
    for load in later:
        load.wait()
    prepare_weights(*held, *made)
    own += fetch(list(zip(made, results)), own_sems, 2)
    for copy in own + copies:
        copy.wait()


def finish_kernel(
    msgs, pos_in, vel_in, types_in, halo_in, coefs_in, out,
    mine, pos, vel, types, halo, coefs, inbox, ring, mixed, box, result,
    slab_out, slab_in, ring_out, ring_in, last_out, last_in, load_sems,
):
    me, peers = slab_peers()
    bead = lax.axis_index("bead")
    z, y = lax.div(bead, NY), lax.rem(bead, NY)

    def along(d):
        return {"bead": lax.rem(z + NZ + d, NZ) * NY + y}

    steps = [d for k in range(1, REACH + 1) for d in (k, -k)]
    ypeers = [{"bead": z * NY + lax.rem(y + k, NY)} for k in range(1, NY)]
    everyone = [along(d) for d in steps[::-1]] + peers + ypeers
    hail(everyone)
    loads = fetch(
        [
            (msgs.at[me], mine), (pos_in, pos), (vel_in, vel), (types_in, types), (halo_in, halo),
            (coefs_in.at[y], coefs),
        ],
        load_sems,
    )
    for load in loads:
        load.wait()
    bins = pltpu.roll(spread_rows(halo[...], 8), 64, 1)[0:1]
    hit = jnp.where(lax.broadcasted_iota(jnp.int32, (LANES, LANES), 0) == bins, 1.0, 0.0)
    meet(everyone)

    copies = [
        send(msgs.at[lax.rem(me + i + 1, N_SLAB)], inbox.at[i], slab_out.at[i], slab_in.at[i], peer)
        for i, peer in enumerate(peers)
    ]
    got = mine[...]
    for i, copy in enumerate(copies):
        copy.wait()
        got = got + inbox[i]
    back = lax.dot_general(got, hit, NT, preferred_element_type=F32, precision=HIGH)
    force = -(got[0:3] + back[3:6])
    kicked = vel[:, 0, :] + STEP * jnp.where(types[...] == 1, 1.0, 1.0 / HEAVY) * force
    own = ring.at[REACH]
    own[...] = jnp.concatenate([pos[:, 0, :], kicked, jnp.zeros((2, LANES), F32)], axis=0)

    near = {
        d: send(own, ring.at[REACH - d], ring_out.at[n], ring_in.at[n], along(d)) for n, d in enumerate(steps)
    }
    result[6:9, 0, :] = force
    for d in steps:
        near[d].wait()
    blocks = jnp.concatenate([ring[n] for n in range(2 * REACH + 1)], axis=0)
    sums = lax.dot_general(
        coefs[...], blocks, (((1,), (0,)), ((), ())), preferred_element_type=F32, precision=HIGH
    )
    copies = []
    for n, (far, k) in enumerate(TARGETS):
        if n != OWN:
            mixed[n] = sums[8 * n : 8 * n + 8]
            peer = {"bead": lax.rem(z + NZ + REACH * far, NZ) * NY + lax.rem(y + k, NY)}
            copies.append((n, send(mixed.at[n], box.at[n], last_out.at[n], last_in.at[n], peer)))
    done = sums[8 * OWN : 8 * OWN + 8]
    for n, copy in copies:
        copy.wait()
        done = done + box[n]
    result[0:6, 0, :] = done[0:6]
    for load in fetch([(result, out)], load_sems):
        load.wait()


TARGETS = [(far, k) for far in (1, 0, -1) for k in range(NY)]
OWN = TARGETS.index((0, 0))


def ring_coefficients():
    cos, travel, spring = (m[:, 0].astype(np.float64) for m in mode_matrices())
    table = np.zeros((NY, 3 * NY, 8, 2 * REACH + 1, 8), np.float32)
    held = {1: range(-REACH, 0), 0: range(-REACH, REACH + 1), -1: range(1, REACH)}
    for y in range(NY):
        for n, (far, k) in enumerate(TARGETS):
            for r in held[far]:
                apart = (NY * (REACH * far - r) + (y + k) % NY - y) % BEADS
                for c in range(3):
                    table[y, n, c, r + REACH, c] = cos[apart]
                    table[y, n, c, r + REACH, 3 + c] = travel[apart]
                    table[y, n, 3 + c, r + REACH, c] = -spring[apart]
                    table[y, n, 3 + c, r + REACH, 3 + c] = cos[apart]
    return table.reshape(NY, 3 * NY * 8, (2 * REACH + 1) * 8)


def dmas(n):
    return pltpu.SemaphoreType.DMA((n,))


def like(x):
    return pltpu.VMEM(x.shape, x.dtype)


def finish_call(msgs, pos, vel, types, halo):
    near = 2 * REACH
    place = pl.BlockSpec(memory_space=PLACE)
    return pl.pallas_call(
        finish_kernel,
        out_shape=jax.ShapeDtypeStruct((9, 1, LANES), F32),
        in_specs=[place] * 6,
        out_specs=place,
        scratch_shapes=[
            pltpu.VMEM((8, LANES), F32),
            like(pos), like(vel), like(types), like(halo),
            pltpu.VMEM((3 * NY * 8, (near + 1) * 8), F32),
            pltpu.VMEM((7, 8, LANES), F32),
            pltpu.VMEM((near + 1, 8, LANES), F32),
            pltpu.VMEM((3 * NY, 8, LANES), F32),
            pltpu.VMEM((3 * NY, 8, LANES), F32),
            pltpu.VMEM((9, 1, LANES), F32),
            dmas(7), dmas(7), dmas(near), dmas(near), dmas(3 * NY), dmas(3 * NY), dmas(6),
        ],
        compiler_params=pltpu.CompilerParams(collective_id=1, has_side_effects=True),
        name="finish",
    )(msgs, pos, vel, types, halo, jnp.asarray(ring_coefficients()))


def local(
    positions, velocities, atom_types, live_atoms, halo_rows, neighbours,
    type_scale, type_shift, embed_two, embed_bias_two, embed_three, embed_bias_three,
    fit_first, fit_bias_first, fit_second, fit_bias_second, fit_third, fit_bias_third, fit_readout,
):
    del live_atoms
    types = atom_types[None]
    s1, a2, p1, a3, p2, _, _ = selections()
    place = pl.BlockSpec(memory_space=PLACE)
    weights = (
        type_scale, type_shift, embed_two, embed_bias_two[None], embed_three, embed_bias_three[None],
        jnp.asarray(s1), jnp.asarray(a2, BF16), jnp.asarray(p1, BF16), jnp.asarray(a3, BF16),
        jnp.asarray(p2, BF16),
    )
    made = (
        jax.ShapeDtypeStruct((56, 32), BF16),
        jax.ShapeDtypeStruct((104, 56), BF16),
        jax.ShapeDtypeStruct((4, 32, LANES), F32),
    )
    firsts = (positions, types, halo_rows)
    tiles, nb, w2t, w3t, cols = pl.pallas_call(
        exchange_kernel,
        out_shape=(
            jax.ShapeDtypeStruct((N_SLAB, 8, LANES), F32),
            jax.ShapeDtypeStruct((N_SLAB, SHARE, LANES), jnp.int32),
        ) + made,
        in_specs=[place] * 15,
        out_specs=(place,) * 5,
        scratch_shapes=[like(x) for x in firsts + weights + made] + [
            pltpu.VMEM((8, LANES), F32), dmas(7), dmas(7), dmas(7), dmas(7), dmas(5), dmas(14),
        ],
        compiler_params=pltpu.CompilerParams(collective_id=0, has_side_effects=True),
        name="exchange",
    )(*firsts, neighbours.reshape(SHARE, N_SLAB, LANES), *weights)
    msgs = force_call(
        tiles, nb, w2t, w3t, cols,
        (fit_first, fit_bias_first, fit_second, fit_bias_second, fit_third, fit_bias_third, fit_readout),
    )
    out = finish_call(msgs, positions, velocities, types, halo_rows)
    return out[0:3], out[3:6], out[6:9]


def solution(mesh):
    wide = P(None, "bead", "slab")
    return jax.shard_map(
        local,
        mesh=mesh,
        in_specs=(wide, wide, P("slab"), P("slab"), P("slab", None), P("slab", None)) + (P(),) * 13,
        out_specs=(wide, wide, wide),
        check_vma=False,
    )
```

```python
import functools

import jax
import jax.numpy as jnp
import numpy as np
from jax import lax
from jax.experimental import pallas as pl
from jax.experimental.pallas import tpu as pltpu
from jax.sharding import PartitionSpec as P

BEADS = 64
N_SLAB = 8
SHARE = 16
LANES = 128
STEP = 0.25
HEAVY = 16.0
BLK = 16
BACK = 32
MXU_GROUPS = 8
CHUNK = 64
F32 = jnp.float32
BF16 = jnp.bfloat16
NT = (((1,), (1,)), ((), ()))
HIGH = lax.Precision.HIGHEST
PLACE = pltpu.HBM


def two_feature(row):
    if row < 24:
        return row
    if row < 48:
        return row + 1
    if row < 52:
        return (24, 49)[(row - 48) % 2]
    return -1


def three_feature(row):
    if row < 48:
        return two_feature(row)
    if row < 96:
        return 50 + two_feature(row - 48)
    if row < 100:
        return (24, 49, 74, 99)[row - 96]
    return -1


def selections():
    one_of = [k if k < 24 else 24 if k < 28 else -1 for k in range(32)]
    s1 = np.zeros((32, 25), np.float32)
    for k, f in enumerate(one_of):
        if f >= 0:
            s1[k, f] = 1
    a2 = np.zeros((56, 50), np.float32)
    for k in range(56):
        if two_feature(k) >= 0:
            a2[k, two_feature(k)] = 1
    b1 = np.zeros((25, 32), np.float32)
    for f in range(25):
        b1[f, f] = 1
    a3 = np.zeros((104, 100), np.float32)
    where = np.zeros((104,), np.int32)
    where[100:] = 127
    for k in range(104):
        if three_feature(k) >= 0:
            a3[k, three_feature(k)] = 1
            where[three_feature(k)] = k
    b2 = np.zeros((50, 56), np.float32)
    for k in range(50):
        b2[two_feature(k), k] = 1
    fold = np.zeros((14 * LANES, LANES), np.float32)
    places = np.full((16, LANES), 127, np.int32)
    for lane in range(1600):
        fold[lane, where[lane // 16]] = 1
        places[lane // LANES, lane % LANES] = where[lane // 16]
    for lane in range(LANES):
        fold[13 * LANES + lane, lane % 16] = 1
    return s1, a2, b1, a3, b2, places, fold


def mode_matrices():
    n = BEADS
    j, k = np.arange(n)[:, None], np.arange(n)[None, :]
    angle = 2 * np.pi * ((j * k) % n) / n
    basis = np.where(
        k == 0,
        1 / np.sqrt(n),
        np.where(
            k < n // 2,
            np.sqrt(2 / n) * np.cos(angle),
            np.where(k == n // 2, np.where(j % 2 == 0, 1.0, -1.0) / np.sqrt(n), np.sqrt(2 / n) * np.sin(angle)),
        ),
    )
    sine = np.sin(np.pi * np.arange(n) / n)
    ratio = 2 * sine
    theta = 1.2 * n * sine
    travel = np.where(np.arange(n) == 0, 1.0, np.sin(theta) / np.where(np.arange(n) == 0, 1.0, ratio))
    return tuple(
        ((basis * d[None, :]) @ basis.T).astype(np.float32)
        for d in (np.cos(theta), travel, ratio * np.sin(theta))
    )


def lanes_of(table, index):
    return jnp.take_along_axis(table, index, axis=1, mode="promise_in_bounds")


def spread_rows(row, count):
    return jnp.broadcast_to(row, (count, row.shape[1]))


def own_tile(pos, types, halo):
    hydrogen = jnp.where(types == 1, 1.0, 0.0).astype(F32)
    mine = jnp.concatenate([pos, hydrogen], axis=0)
    wide = jnp.concatenate([mine, mine], axis=0)
    sent = lanes_of(wide, spread_rows(halo, 8))
    return jnp.where(lax.broadcasted_iota(jnp.int32, (8, LANES), 0) < 4, wide, sent)


def thirds(row):
    high = row.astype(BF16).astype(F32)
    rest = row - high
    mid = rest.astype(BF16).astype(F32)
    return high, mid, rest - mid


def bias_rows(bias, first, count):
    high, mid, low = thirds(bias)
    at = lax.broadcasted_iota(jnp.int32, (count, bias.shape[1]), 0)
    return jnp.where(at == first, high, jnp.where(at == first + 1, mid, jnp.where(at == first + 2, low, 0.0)))


def prepare_weights(scale, shift, w2, b2, w3, b3, s1, a2, p1, a3, p2, w2t, w3t, cols):
    dot = functools.partial(lax.dot_general, preferred_element_type=F32)
    two = dot(a2[...], w2[...], NT).astype(BF16)
    two = dot(two, p1[...], (((1,), (0,)), ((), ())))
    two = two + dot(a2[...], bias_rows(b2[...], 28, 32).astype(BF16), NT)
    w2t[...] = two.astype(BF16)
    three = dot(a3[...], w3[...], NT).astype(BF16)
    three = dot(three, p2[...], (((1,), (0,)), ((), ())))
    three = three + dot(a3[...], bias_rows(b3[...], 52, 56).astype(BF16), NT)
    w3t[...] = three.astype(BF16)
    at = lax.broadcasted_iota(jnp.int32, (32, LANES), 0)
    ones = jnp.where((at >= 28) & (at < 31), 20.0, 0.0)
    for kind in range(2):
        for n, ref in enumerate((scale, shift)):
            col = dot(s1[...], spread_rows(ref[kind : kind + 1, :], LANES), NT, precision=HIGH)
            cols[2 * n + kind] = col + ones if n else col


def fetch(pairs, sems, first=0):
    loads = [pltpu.make_async_copy(src, dst, sems.at[first + n]) for n, (src, dst) in enumerate(pairs)]
    for load in loads:
        load.start()
    return loads


def force_kernel(*refs):
    given, out, held, rest = refs[:14], refs[14], refs[15:29], refs[29:]
    (
        tile, nb, w2t, w3t, cols, places, c1, c2, c3, readout, fit1, fit2, fit3, fold,
    ) = held
    env, geo, order, count, hc, three, feats, gfeats, qs, ps, scat, sems = rest
    me = lax.axis_index("slab")
    loads = fetch(list(zip(given, held)), sems)
    for load in loads[:2]:
        load.wait()
    dot = functools.partial(lax.dot_general, preferred_element_type=F32)
    NN = (((1,), (0,)), ((), ()))
    lane8 = lax.broadcasted_iota(jnp.int32, (8, LANES), 1)
    row8 = lax.broadcasted_iota(jnp.int32, (8, LANES), 0)

    for s in range(N_SLAB):
        count[s] = jnp.sum(jnp.where(nb[s][:, 0:1] >= 0, 1.0, 0.0)).astype(jnp.int32)
    total = jnp.int32(0)
    for s in range(N_SLAB):
        for j in range(SHARE):
            order[total + j] = s * SHARE + j
        total = total + count[s]
    for j in range(max(BLK, BACK)):
        order[total + j] = N_SLAB * SHARE
    env[pl.ds(N_SLAB * SHARE * 8, 8), :] = jnp.zeros((8, LANES), F32)

    def own_row(s, half):
        return (row8 + half * 8) * 8 + lax.rem(me - s + N_SLAB, N_SLAB)

    def geometry(s, half):
        before = lax.rem(s + N_SLAB - 1, N_SLAB)
        after = lax.rem(s + 1, N_SLAB)
        idx = nb[s, half * 8 : half * 8 + 8, :]
        low = idx & 127
        far = idx >= 128
        own = tile[s]
        edge = pltpu.roll(jnp.where(lane8 >= 64, tile[before], tile[after]), 64, 1)
        centre_at = own_row(s, half)
        base = s * SHARE + half * 8
        got = []
        for c in range(4):
            near = lanes_of(spread_rows(own[c : c + 1], 8), low)
            there = lanes_of(spread_rows(edge[4 + c : 5 + c], 8), low)
            got.append(jnp.where(far, there, near))
        mid = [lanes_of(spread_rows(own[c : c + 1], 8), centre_at) for c in range(4)]
        off = [got[c] - mid[c] for c in range(3)]
        d2 = off[0] * off[0] + off[1] * off[1] + off[2] * off[2]
        inv = lax.rsqrt(d2 + 0.25)
        fsw = jnp.where(idx >= 0, jnp.maximum(1.0 - d2 * (1.0 / 16.0), 0.0), 0.0)
        strength = fsw * fsw * inv
        si = strength * inv
        at = pl.ds(base, 8)
        for n, value in enumerate((*off, inv, fsw)):
            geo[n, at, :] = value
        for n, value in enumerate((strength, si * off[0], si * off[1], si * off[2], got[3], mid[3])):
            env[pl.ds(base * 8 + n, 8, stride=8), :] = value

    for s in range(N_SLAB):
        geometry(s, 0)

    def second_half(fn):
        def step(s, carry):
            @pl.when(count[s] > 8)
            def _():
                fn(s, 1)
            return carry

        lax.fori_loop(0, N_SLAB, step, 0)

    second_half(geometry)

    for load in loads[2:6]:
        load.wait()
    sc0, sc1, sh0, sh1 = 0, 1, 2, 3

    def forward(first, size):
        e, one, done = [], [], []
        for b in range(size):
            row = order[first + b]
            v = env[pl.ds(pl.multiple_of(row * 8, 8), 8), :]
            e.append(v)
            hyd = v[4:5] > 0.5
            sc = jnp.where(hyd, cols[sc1], cols[sc0])
            t = jnp.tanh(v[0:1] * sc + jnp.where(hyd, cols[sh1], cols[sh0]))
            one.append((t, (1.0 - t * t) * sc))
            hc[pl.ds(first + b, 1), :] = v[5:6]
        x = jnp.concatenate([a.astype(BF16) for pair in one for a in pair], axis=1)
        z = dot(w2t[...], x, NN)
        two = []
        for b in range(size):
            t1, d1 = one[b]
            t = jnp.tanh(z[:, 256 * b : 256 * b + 128])
            d = (1.0 - t * t) * z[:, 256 * b + 128 : 256 * b + 256]
            two.append((
                (t + jnp.concatenate([t1[:24], t1[:24], t1[24:]], axis=0)).astype(BF16),
                (d + jnp.concatenate([d1[:24], d1[:24], d1[24:]], axis=0)).astype(BF16),
            ))
        x = jnp.concatenate([a for pair in two for a in pair], axis=1)
        z = dot(w3t[...], x, NN)
        for b in range(size):
            t2, d2 = two[b]
            t = jnp.tanh(z[:, 256 * b : 256 * b + 128].astype(BF16))
            d = (1 - t * t) * z[:, 256 * b + 128 : 256 * b + 256].astype(BF16)
            l3 = t + jnp.concatenate([t2[:48], t2[:48], t2[48:]], axis=0)
            d3 = d + jnp.concatenate([d2[:48], d2[:48], d2[48:]], axis=0)
            three[first + b] = jnp.concatenate([l3, d3], axis=1)
            f = dot(e[b].astype(BF16), l3, NT) * (1.0 / 128.0)
            feats[pl.ds(pl.multiple_of((first + b) * 8, 8), 8), :] = jnp.concatenate(
                [f, jnp.zeros((8, 24), F32)], axis=1
            )

    full = lax.div(total + (BLK // 2 - 1), BLK)

    def whole_step(block, carry):
        forward(block * BLK, BLK)
        return carry

    def half_step(block, carry):
        forward(full * BLK, BLK // 2)
        return carry

    lax.fori_loop(0, full, whole_step, 0)
    lax.fori_loop(0, jnp.where(total > full * BLK, 1, 0), half_step, 0)

    for load in loads[6:]:
        load.wait()

    lane_m = lax.broadcasted_iota(jnp.int32, (CHUNK, LANES), 1)

    def fit(chunk, carry):
        base = chunk * (CHUNK * 8)
        fs = [feats[pl.ds(base + c, CHUNK, stride=8), :] for c in range(4)]
        stack = jnp.concatenate(fs, axis=0).astype(BF16)
        picks = dot(stack, fold[: MXU_GROUPS * LANES], NT)
        tiled = [lanes_of(f, lane_m & 15) for f in fs]
        spreads = [
            [picks[CHUNK * c : CHUNK * (c + 1), g * LANES : (g + 1) * LANES] for g in range(MXU_GROUPS)]
            + [lanes_of(fs[c], spread_rows(places[g : g + 1, :], CHUNK)) for g in range(MXU_GROUPS, 13)]
            for c in range(4)
        ]
        desc = [sum(spreads[c][g] * tiled[c] for c in range(4)).astype(BF16) for g in range(13)]
        desc = jnp.concatenate(desc, axis=1)[:, :1600]
        short = [v.astype(BF16) for v in tiled]
        f1 = jnp.tanh(dot(desc, fit1[...], NT) + c1[...])
        t2 = jnp.tanh(dot(f1.astype(BF16), fit2[...], NN) + c2[...])
        f2 = t2 + f1
        t3 = jnp.tanh(dot(f2.astype(BF16), fit3[...], NN) + c3[...])
        h = hc[pl.ds(chunk * CHUNK, CHUNK), :]
        h = jnp.concatenate([h, h], axis=1)[:, :240]
        g3 = readout[0:1, :] + h * (readout[1:2, :] - readout[0:1, :])
        g2 = g3 + dot((g3 * (1.0 - t3 * t3)).astype(BF16), fit3[...], NT)
        g1 = g2 + dot((g2 * (1.0 - t2 * t2)).astype(BF16), fit2[...], NT)
        gd = dot((g1 * (1.0 - f1 * f1)).astype(BF16), fit1[...], NN)
        gd = jnp.concatenate([gd, jnp.zeros((CHUNK, 64), F32)], axis=1)
        parts = [gd[:, g * LANES : (g + 1) * LANES] for g in range(13)]
        left = [jnp.concatenate([p.astype(BF16) * v for p in parts], axis=1) for v in short]
        gf = dot(jnp.concatenate(left, axis=0), fold[: 13 * LANES], NN)
        right = [sum(parts[g] * spreads[c][g] for g in range(13)) for c in range(4)]
        gf = gf + dot(jnp.concatenate(right, axis=0).astype(BF16), fold[13 * LANES :], NN)
        for c in range(4):
            part = gf[CHUNK * c : CHUNK * (c + 1)] * (1.0 / 128.0)
            gfeats[pl.ds(base + c, CHUNK, stride=8), :] = part
        return carry

    lax.fori_loop(0, lax.div(total + (CHUNK - 1), CHUNK), fit, 0)

    def back(block, carry):
        first = block * BACK
        for b in range(BACK):
            row = order[first + b]
            gf = gfeats[pl.ds(pl.multiple_of((first + b) * 8, 8), 8), :][:, :104]
            qp = dot(gf.astype(BF16), three[first + b], NN)
            at = pl.ds(pl.multiple_of(row * 8, 8), 8)
            qs[at, :] = qp[:, :128]
            ps[at, :] = qp[:, 128:]
        return carry

    lax.fori_loop(0, lax.div(total + (BACK - 1), BACK), back, 0)

    sub = lax.broadcasted_iota(jnp.int32, (LANES, LANES), 0).astype(F32).astype(BF16)

    def scatter(s, half):
        base = s * SHARE + half * 8
        at = pl.ds(base, 8)
        idx = nb[s, half * 8 : half * 8 + 8, :]
        off = [geo[n, at, :] for n in range(3)]
        inv, fsw = geo[3, at, :], geo[4, at, :]
        q = [qs[pl.ds(base * 8 + n, 8, stride=8), :] for n in range(4)]
        p = [ps[pl.ds(base * 8 + n, 8, stride=8), :] for n in range(4)]
        inv3 = 0.5 * inv * inv * inv
        strength = fsw * fsw * inv
        qo = q[1] * off[0] + q[2] * off[1] + q[3] * off[2]
        po = p[1] * off[0] + p[2] * off[1] + p[3] * off[2]
        gs = q[0] + inv * qo + strength * (p[0] + inv * po)
        gd2 = -gs * (fsw * inv * 0.125 + fsw * fsw * inv3) - qo * strength * inv3
        si = strength * inv
        g = [jnp.where(idx >= 0, q[1 + c] * si + 2.0 * off[c] * gd2, 0.0) for c in range(3)]
        near = idx < 128
        centre_at = own_row(s, half) == lane8
        grad = jnp.zeros((8, LANES), F32)
        for c in range(3):
            scat[pl.ds(base * 8 + c, 8, stride=8), :] = jnp.where(near, g[c], 0.0)
            scat[pl.ds(base * 8 + 3 + c, 8, stride=8), :] = jnp.where(near, 0.0, g[c])
            total_c = jnp.sum(g[c], axis=1, keepdims=True)
            line = jnp.sum(jnp.where(centre_at, -total_c, 0.0), axis=0, keepdims=True)
            grad = jnp.where(row8 == c, line, grad)
        lhs, rhs = [], []
        for j in range(8):
            lhs.append(scat[pl.ds((base + j) * 8, 8), :].astype(BF16))
            low = nb[s, half * 8 + j : half * 8 + j + 1, :] & 127
            low = spread_rows(low.astype(F32).astype(BF16), LANES)
            rhs.append(jnp.where(sub == low, jnp.ones_like(sub), jnp.zeros_like(sub)))
        grad = grad + dot(jnp.concatenate(lhs, axis=1), jnp.concatenate(rhs, axis=1), NT)
        if half == 0:
            feats[pl.ds(s * 8, 8), :] = grad
        else:
            feats[pl.ds(s * 8, 8), :] += grad

    for s in range(N_SLAB):
        scatter(s, 0)
    second_half(scatter)
    grads = [feats[pl.ds(s * 8, 8), :] for s in range(N_SLAB)]
    for s in range(N_SLAB):
        edge = jnp.where(lane8 < 64, grads[(s + 1) % N_SLAB], grads[(s - 1) % N_SLAB])
        out[s] = jnp.where(row8 < 3, grads[s], edge)


def force_call(tile, nb, w2t, w3t, cols, fit):
    fit1, b1, fit2, b2, fit3, b3, readout = fit
    places, fold = selections()[-2:]
    rows = N_SLAB * SHARE
    operands = (
        tile, nb, w2t, w3t, cols, jnp.asarray(places), b1[None], b2[None], b3[None], readout,
        fit1.T, fit2, fit3, jnp.asarray(fold, BF16),
    )
    return pl.pallas_call(
        force_kernel,
        out_shape=jax.ShapeDtypeStruct((N_SLAB, 8, LANES), F32),
        in_specs=[pl.BlockSpec(memory_space=PLACE)] * len(operands),
        out_specs=pl.BlockSpec(memory_space=pltpu.VMEM),
        scratch_shapes=[pltpu.VMEM(x.shape, x.dtype) for x in operands] + [
            pltpu.VMEM(((rows + 1) * 8, LANES), F32),
            pltpu.VMEM((5, rows, LANES), F32),
            pltpu.SMEM((rows + 48,), jnp.int32),
            pltpu.SMEM((N_SLAB,), jnp.int32),
            pltpu.VMEM((rows + 32, LANES), F32),
            pltpu.VMEM((rows + 32, 104, 256), BF16),
            pltpu.VMEM(((rows + 32) * 8, LANES), F32),
            pltpu.VMEM(((rows + 32) * 8, LANES), F32),
            pltpu.VMEM(((rows + 1) * 8, LANES), F32),
            pltpu.VMEM(((rows + 1) * 8, LANES), F32),
            pltpu.VMEM((rows * 8, LANES), F32),
            pltpu.SemaphoreType.DMA((len(operands),)),
        ],
        name="force",
    )(*operands)


MESH = pl.DeviceIdType.MESH
NZ = 16
NY = 4
REACH = 4


def hail(peers):
    barrier = pltpu.get_barrier_semaphore()
    for peer in peers:
        pl.semaphore_signal(barrier, inc=1, device_id=peer, device_id_type=MESH)


def meet(peers):
    pl.semaphore_wait(pltpu.get_barrier_semaphore(), len(peers))


def send(src, dst, out_sem, in_sem, peer):
    copy = pltpu.make_async_remote_copy(
        src_ref=src, dst_ref=dst, send_sem=out_sem, recv_sem=in_sem, device_id=peer, device_id_type=MESH
    )
    copy.start()
    return copy


def slab_peers():
    me = lax.axis_index("slab")
    return me, [{"slab": lax.rem(me + i, N_SLAB)} for i in range(1, N_SLAB)]


def exchange_kernel(*refs):
    pos_in, types_in, halo_in, lists = refs[:4]
    weights, (tiles, nb), results = refs[4:15], refs[15:17], refs[17:20]
    pos, types, halo = refs[20:23]
    held, made, mine = refs[23:34], refs[34:37], refs[37]
    tile_out, tile_in, list_out, list_in, own_sems, load_sems = refs[38:]
    me, peers = slab_peers()
    hail(peers)
    first = fetch([(pos_in, pos), (types_in, types), (halo_in, halo)], load_sems)
    later = fetch(list(zip(weights, held)), load_sems, 3)
    for load in first:
        load.wait()
    mine[...] = own_tile(pos[:, 0, :], types[...], halo[...])
    meet(peers)
    copies = []
    for i, peer in enumerate(peers):
        copies.append(send(lists.at[:, i + 1, :], nb.at[me], list_out.at[i], list_in.at[i], peer))
    for i, peer in enumerate(peers):
        copies.append(send(mine, tiles.at[me], tile_out.at[i], tile_in.at[i], peer))
    own = fetch([(lists.at[:, 0, :], nb.at[me]), (mine, tiles.at[me])], own_sems)
    for load in later:
        load.wait()
    prepare_weights(*held, *made)
    own += fetch(list(zip(made, results)), own_sems, 2)
    for copy in own + copies:
        copy.wait()


def halves(x):
    high = x.astype(BF16)
    return high, (x - high.astype(F32)).astype(BF16)


def finish_kernel(
    msgs, pos_in, vel_in, types_in, halo_in, coefs_in, out,
    mine, pos, vel, types, halo, coefs, inbox, ring, mixed, box, result,
    slab_out, slab_in, ring_out, ring_in, last_out, last_in, load_sems,
):
    me, peers = slab_peers()
    bead = lax.axis_index("bead")
    z, y = lax.div(bead, NY), lax.rem(bead, NY)

    def along(d):
        return {"bead": lax.rem(z + NZ + d, NZ) * NY + y}

    steps = [d for k in range(REACH, 0, -1) for d in (k, -k)]
    used = pl.ds(0, 6)
    ypeers = [{"bead": z * NY + lax.rem(y + k, NY)} for k in range(1, NY)]
    everyone = [along(d) for d in steps] + peers + ypeers
    hail(everyone)
    loads = fetch(
        [
            (msgs.at[me], mine), (pos_in, pos), (vel_in, vel), (types_in, types), (halo_in, halo),
            (coefs_in.at[y], coefs),
        ],
        load_sems,
    )
    for load in loads:
        load.wait()
    bins = pltpu.roll(spread_rows(halo[...], 8), 64, 1)[0:1]
    hit = jnp.where(lax.broadcasted_iota(jnp.int32, (LANES, LANES), 0) == bins, 1.0, 0.0).astype(BF16)
    meet(everyone)

    copies = [
        send(msgs.at[lax.rem(me + i + 1, N_SLAB), used], inbox.at[i], slab_out.at[i], slab_in.at[i], peer)
        for i, peer in enumerate(peers)
    ]
    got = mine[0:6, :]
    for i, copy in enumerate(copies):
        copy.wait()
        got = got + inbox[i]
    high, low = halves(got)
    dot = functools.partial(lax.dot_general, preferred_element_type=F32)
    back = dot(high, hit, NT) + dot(low, hit, NT)
    force = -(got[0:3] + back[3:6])
    kicked = vel[:, 0, :] + STEP * jnp.where(types[...] == 1, 1.0, 1.0 / HEAVY) * force
    own = ring.at[REACH]
    own[...] = jnp.concatenate([pos[:, 0, :], kicked], axis=0)

    near = {
        d: send(own, ring.at[REACH - d], ring_out.at[n], ring_in.at[n], along(d)) for n, d in enumerate(steps)
    }
    result[6:9, 0, :] = force
    for d in steps:
        near[d].wait()
    blank = jnp.zeros((2, LANES), F32)
    blocks = [x for n in range(2 * REACH + 1) for x in (ring[n], blank)] + [jnp.zeros((8, LANES), F32)]
    high, low = halves(jnp.concatenate(blocks, axis=0))
    sums = dot(coefs[...], jnp.concatenate([high, high, low], axis=0), (((1,), (0,)), ((), ())))
    copies = []
    for n, (far, k) in enumerate(TARGETS):
        if n != OWN:
            mixed[n] = sums[8 * n : 8 * n + 6]
            peer = {"bead": lax.rem(z + NZ + REACH * far, NZ) * NY + lax.rem(y + k, NY)}
            copies.append((n, send(mixed.at[n], box.at[n], last_out.at[n], last_in.at[n], peer)))
    done = sums[8 * OWN : 8 * OWN + 6]
    for n, copy in copies:
        copy.wait()
        done = done + box[n]
    result[0:6, 0, :] = done
    for load in fetch([(result, out)], load_sems):
        load.wait()


TARGETS = [(far, k) for k in (2, 1, 3, 0) for far in (1, -1)] + [(0, k) for k in (2, 1, 3, 0)]
OWN = TARGETS.index((0, 0))


def ring_coefficients():
    cos, travel, spring = (m[:, 0].astype(np.float64) for m in mode_matrices())
    table = np.zeros((NY, 3 * NY, 8, 2 * REACH + 1, 8), np.float32)
    held = {1: range(-REACH, 0), 0: range(-REACH, REACH + 1), -1: range(1, REACH)}
    for y in range(NY):
        for n, (far, k) in enumerate(TARGETS):
            for r in held[far]:
                apart = (NY * (REACH * far - r) + (y + k) % NY - y) % BEADS
                for c in range(3):
                    table[y, n, c, r + REACH, c] = cos[apart]
                    table[y, n, c, r + REACH, 3 + c] = travel[apart]
                    table[y, n, 3 + c, r + REACH, c] = -spring[apart]
                    table[y, n, 3 + c, r + REACH, 3 + c] = cos[apart]
    table = table.reshape(NY, 3 * NY * 8, (2 * REACH + 1) * 8)
    table = np.pad(table, ((0, 0), (0, 0), (0, 8)))
    high = table.astype(jnp.bfloat16)
    low = (table - high.astype(np.float32)).astype(jnp.bfloat16)
    return np.concatenate([high, low, high], axis=2)


def dmas(n):
    return pltpu.SemaphoreType.DMA((n,))


def like(x):
    return pltpu.VMEM(x.shape, x.dtype)


def finish_call(msgs, pos, vel, types, halo):
    near = 2 * REACH
    place = pl.BlockSpec(memory_space=PLACE)
    return pl.pallas_call(
        finish_kernel,
        out_shape=jax.ShapeDtypeStruct((9, 1, LANES), F32),
        in_specs=[place] * 6,
        out_specs=place,
        scratch_shapes=[
            pltpu.VMEM((8, LANES), F32),
            like(pos), like(vel), like(types), like(halo),
            pltpu.VMEM((3 * NY * 8, 3 * (near + 2) * 8), BF16),
            pltpu.VMEM((7, 6, LANES), F32),
            pltpu.VMEM((near + 1, 6, LANES), F32),
            pltpu.VMEM((3 * NY, 6, LANES), F32),
            pltpu.VMEM((3 * NY, 6, LANES), F32),
            pltpu.VMEM((9, 1, LANES), F32),
            dmas(7), dmas(7), dmas(near), dmas(near), dmas(3 * NY), dmas(3 * NY), dmas(6),
        ],
        compiler_params=pltpu.CompilerParams(collective_id=1, has_side_effects=True),
        name="finish",
    )(msgs, pos, vel, types, halo, jnp.asarray(ring_coefficients()))


def local(
    positions, velocities, atom_types, live_atoms, halo_rows, neighbours,
    type_scale, type_shift, embed_two, embed_bias_two, embed_three, embed_bias_three,
    fit_first, fit_bias_first, fit_second, fit_bias_second, fit_third, fit_bias_third, fit_readout,
):
    del live_atoms
    types = atom_types[None]
    s1, a2, p1, a3, p2, _, _ = selections()
    place = pl.BlockSpec(memory_space=PLACE)
    weights = (
        type_scale, type_shift, embed_two, embed_bias_two[None], embed_three, embed_bias_three[None],
        jnp.asarray(s1), jnp.asarray(a2, BF16), jnp.asarray(p1, BF16), jnp.asarray(a3, BF16),
        jnp.asarray(p2, BF16),
    )
    made = (
        jax.ShapeDtypeStruct((56, 32), BF16),
        jax.ShapeDtypeStruct((104, 56), BF16),
        jax.ShapeDtypeStruct((4, 32, LANES), F32),
    )
    firsts = (positions, types, halo_rows)
    tiles, nb, w2t, w3t, cols = pl.pallas_call(
        exchange_kernel,
        out_shape=(
            jax.ShapeDtypeStruct((N_SLAB, 8, LANES), F32),
            jax.ShapeDtypeStruct((N_SLAB, SHARE, LANES), jnp.int32),
        ) + made,
        in_specs=[place] * 15,
        out_specs=(place,) * 5,
        scratch_shapes=[like(x) for x in firsts + weights + made] + [
            pltpu.VMEM((8, LANES), F32), dmas(7), dmas(7), dmas(7), dmas(7), dmas(5), dmas(14),
        ],
        compiler_params=pltpu.CompilerParams(collective_id=0, has_side_effects=True),
        name="exchange",
    )(*firsts, neighbours.reshape(SHARE, N_SLAB, LANES), *weights)
    msgs = force_call(
        tiles, nb, w2t, w3t, cols,
        (fit_first, fit_bias_first, fit_second, fit_bias_second, fit_third, fit_bias_third, fit_readout),
    )
    out = finish_call(msgs, positions, velocities, types, halo_rows)
    return out[0:3], out[3:6], out[6:9]


def solution(mesh):
    wide = P(None, "bead", "slab")
    return jax.shard_map(
        local,
        mesh=mesh,
        in_specs=(wide, wide, P("slab"), P("slab"), P("slab", None), P("slab", None)) + (P(),) * 13,
        out_specs=(wide, wide, wide),
        check_vma=False,
    )
```
